256 devices in a mesh: brick: 64 (over y, z, core), grp: 4 (over x).
Axes of the slice: x: 4, y: 4, z: 8, core: 2. Of those that a mesh axis runs over, the one named last changes fastest.
Arguments:
- gradients: bfloat16 [512, 1048576], P('grp', 'brick'), may hold values from -33 to 33
- perm: int32 [8192], replicated, may hold values from 0 to 8191, as said below
- weights: float32 [1048576], P(('brick', 'grp')), may hold values from 0.1 to 48
- linear: float32 [1048576], P(('brick', 'grp')), may hold values from -6 to 6
- bound: float32 [512], replicated, may hold values from -0.3 to 0.3
Outputs:
- design_step: float32 [1048576], P(('brick', 'grp'))
- multipliers: float32 [512], replicated
The draws below stay inside these ranges and needn't reach their ends.
Inputs may be any that keep to these rules, and one draw needn't show every extreme that they name: Design block k is the brick-layout block perm[k]; every value appears once. The 128 design blocks of each brick index (the blocks of one index of brick in design layout) come equally, 2 each, from the blocks of every brick index in brick layout.
All inputs are finite; a program needn't handle non-finite values.
Results may differ from the reference program's by a relative error of at most 0.0041.
Values may be sent and summed in bfloat16 or wider, within the bound.
No kernel may reach another device: no remote copies, remote signals or barrier semaphores. Data moves between devices by JAX's collectives and lax.ppermute only.
A program may use at most 64 MiB of HBM per device.

```python
import jax
import jax.numpy as jnp
from jax import lax

M = 512
CD = 4096
ITERS = 4
NVAR = 1048576
NBLK = 8192
N_BRICK = 64
DEVICES = 256


def draw_gradients(key, part):
    first = jax.random.fold_in(key, 11)
    second = jax.random.fold_in(key, 12)
    clusters = max(M // 16, 1)
    shared = jax.random.truncated_normal(second, -4.0, 4.0, (clusters, NVAR), jnp.float32)
    mixed = jnp.repeat(shared, M // clusters, axis=0)
    base = jax.random.truncated_normal(first, -4.0, 4.0, (M, NVAR), jnp.float32)
    result = base + 0.6 * mixed
    return result.astype(jnp.bfloat16)


def draw_weights(key, part):
    first = jax.random.fold_in(key, 31)
    second = jax.random.fold_in(key, 32)
    logs = jax.random.uniform(first, (NVAR,), jnp.float32, jnp.log(0.1), jnp.log(2.0))
    chosen = jax.random.randint(second, (), 0, DEVICES)
    owner = jnp.arange(NVAR, dtype=jnp.int32) // CD
    factor = jnp.where(owner == chosen, 24.0, 1.0).astype(jnp.float32)
    return (jnp.exp(logs) * factor).astype(jnp.float32)


def draw_perm(key, part):
    per_brick = NBLK // N_BRICK
    share = per_brick // N_BRICK
    source_keys = jax.random.split(jax.random.fold_in(key, 21), N_BRICK)
    local = jax.vmap(lambda k: jax.random.permutation(k, per_brick))(source_keys)
    local = local.astype(jnp.int32) + (jnp.arange(N_BRICK, dtype=jnp.int32) * per_brick)[:, None]
    grouped = local.reshape(N_BRICK, N_BRICK, share)
    arranged = jnp.transpose(grouped, (1, 0, 2)).reshape(N_BRICK, per_brick)
    target_keys = jax.random.split(jax.random.fold_in(key, 22), N_BRICK)
    shuffles = jax.vmap(lambda k: jax.random.permutation(k, per_brick))(target_keys).astype(jnp.int32)
    placed = jnp.take_along_axis(arranged, shuffles, axis=1)
    return placed.reshape(NBLK).astype(jnp.int32)


def block_scale(rng, shape, shards, low, high):
    def one(dim, blocks):
        steps = jax.random.uniform(jax.random.fold_in(jax.random.fold_in(rng, 6), dim), (blocks,), jnp.float32, low / len(shards), high / len(shards))
        return jnp.repeat(jnp.exp(steps), shape[dim] // blocks).reshape((-1,) + (1,) * (len(shape) - dim - 1))

    gain = one(*shards[0])
    for cut in shards[1:]:
        gain = gain * one(*cut)
    return gain


def noise(own_key, shape, scale, reach, cuts=(), kind=jnp.bfloat16):
    loudness = block_scale(own_key, shape, cuts, -0.22, 0.18) if cuts else 1.0
    array = jax.random.normal(own_key, shape, jnp.float32) * scale * loudness
    return jnp.minimum(jnp.maximum(array, -reach), reach).astype(kind)


def setup_inputs(seed: int = 0) -> dict:
    splits = jax.random.split(jax.random.key(seed), 6)
    return {
        "gradients": draw_gradients(jax.random.fold_in(splits[5], 71), 0),
        "perm": draw_perm(jax.random.fold_in(splits[5], 71), 0),
        "weights": draw_weights(jax.random.fold_in(splits[5], 71), 0),
        "linear": noise(splits[3], (NVAR,), 1.0, 6.0, ((0, 256),), jnp.float32),
        "bound": noise(splits[4], (M,), 0.05, 0.3, (), jnp.float32),
    }


move_limit = 1.0

def reference(gradients, perm, weights, linear, bound):
    blocks = gradients.reshape(M, NBLK, 128)
    span = min(128, NBLK)
    width = span * 128
    count = NBLK // span

    def pieces(index):
        ids = lax.dynamic_slice_in_dim(perm, (index * span).astype(jnp.int32), span)
        part = jnp.take(blocks, ids, axis=1).reshape(M, width)
        start = (index * width).astype(jnp.int32)
        return (part, lax.dynamic_slice_in_dim(weights, start, width), lax.dynamic_slice_in_dim(linear, start, width))

    def trial(part, curv, lin, lam_b):
        pushed = jnp.dot(lam_b.astype(jnp.float32), part.astype(jnp.float32), preferred_element_type=jnp.float32)
        return jnp.clip(-curv * (lin + pushed), -move_limit, move_limit)

    def gram_step(index, total):
        part, curv, lin = pieces(index)
        weighted = (part.astype(jnp.float32) * curv).astype(jnp.bfloat16)
        return total + lax.dot_general(weighted.astype(jnp.float32), part.astype(jnp.float32), (((1,), (1,)), ((), ())), preferred_element_type=jnp.float32)
    gram = lax.fori_loop(0, count, gram_step, jnp.zeros((M, M), jnp.float32))
    hessian = gram / NVAR
    chol = jnp.linalg.cholesky(0.5 * (hessian + hessian.T))
    lam = jnp.zeros((M,), jnp.float32)
    for step in range(ITERS):
        lam_b = lam.astype(jnp.bfloat16)

        def product_step(index, total):
            part, curv, lin = pieces(index)
            moved = trial(part, curv, lin, lam_b).astype(jnp.bfloat16)
            return total + jnp.dot(part.astype(jnp.float32), moved.astype(jnp.float32), preferred_element_type=jnp.float32)
        product = lax.fori_loop(0, count, product_step, jnp.zeros((M,), jnp.float32))
        lam = jnp.maximum(lam + jax.scipy.linalg.cho_solve((chol, True), product / NVAR - bound), 0.0)
    lam_b = lam.astype(jnp.bfloat16)

    def final_step(index, result):
        part, curv, lin = pieces(index)
        return lax.dynamic_update_slice_in_dim(result, trial(part, curv, lin, lam_b), (index * width).astype(jnp.int32), 0)
    design_step = lax.fori_loop(0, count, final_step, jnp.zeros((NVAR,), jnp.float32))
    return (design_step, lam)
```

```python
import functools

import jax
import jax.numpy as jnp
from jax import lax
from jax.experimental import pallas as pl
from jax.experimental.pallas import tpu as pltpu
from jax.sharding import Mesh
from jax.sharding import PartitionSpec as P

ITERS = 4
BRICK = ("brick_0", "brick_1", "brick_2")
BRICK_GRP = ("brick_0", "brick_1", "brick_2", "grp")
FAR = ("brick_0", "brick_1")
NEAR = ("brick_2", "grp")
PLANE = ("brick_0", "grp")
M = 512
ROWS = 128
NB = M // ROWS
COLS = 4096
BLKS = COLS // 128
NVAR = 1048576
PAIRS = [(i, j) for i in range(NB) for j in range(i + 1)]
SHARDS = 32
SHARD_G = len(PAIRS) * ROWS // SHARDS
SHARD = SHARD_G + 8
HALF = SHARDS // 2
DOUBLINGS = 5
MAX_CORRECT = 48
ACCEPT = 0.01

move_limit = 1.0
MIB = 1024 * 1024
BF = jnp.bfloat16
F32 = jnp.float32


def size_of(axis):
    return lax.axis_size(axis)


def from_everyone(array, axis):
    devices = size_of(axis)
    return lax.all_to_all(
        jnp.broadcast_to(array[None], (devices, *array.shape)), axis, 0, 0, tiled=True
    )


def layout_tables(perm, here, per_brick):
    total_blocks = perm.shape[0]
    index = jnp.arange(total_blocks, dtype=jnp.int32)
    owner = perm // per_brick
    keys = jnp.where(owner == here, index, index + total_blocks)
    chosen = jnp.argsort(keys)[:per_brick]
    outgoing = perm[chosen] % per_brick
    mine = lax.dynamic_slice_in_dim(perm, here * per_brick, per_brick)
    source = mine // per_brick
    arrival = jnp.argsort(source * per_brick + jnp.arange(per_brick, dtype=jnp.int32))
    place = jnp.argsort(arrival)
    return (outgoing, arrival, place)


def down(row):
    return jnp.broadcast_to(row, (128, 128)).T


def times(mat_ref, vec):
    total = [jnp.zeros((8, 128), F32) for _ in range(NB)]
    for i in range(NB):
        column = down(vec[i : i + 1, :])
        for j in range(NB):
            part = mat_ref[i * 128 : (i + 1) * 128, j * 128 : (j + 1) * 128] * column
            total[j] = total[j] + part.reshape(16, 8, 128).sum(axis=0)
    return jnp.concatenate([t.sum(axis=0, keepdims=True) for t in total], axis=0)


def flat_rows(ref, rows, first, count):
    return jnp.concatenate([ref[pl.ds(first + k, 1), :] for k in range(count)], axis=1)


def trial_chunk(full_ref, curv_ref, lin_ref, lam_b, chunk, width):
    count = width // 128
    start = pl.multiple_of(chunk * width, width)
    block = full_ref[:, :, pl.ds(start, width)].reshape(M, width)
    pushed = jnp.dot(lam_b, block, preferred_element_type=F32)
    curv = flat_rows(curv_ref, None, chunk * count, count)
    lin = flat_rows(lin_ref, None, chunk * count, count)
    return jnp.clip(-curv * (lin + pushed), -move_limit, move_limit), block


def as_rows(lam):
    flat = jnp.concatenate([lam[i : i + 1, :] for i in range(NB)], axis=1)
    return jnp.broadcast_to(flat, (16, M)).astype(BF)


def product_of_trial(full_ref, curv_ref, lin_ref, lam, acc_ref):
    width = 1024
    lam_b = as_rows(lam)
    acc_ref[...] = jnp.zeros_like(acc_ref)

    def step(chunk, carry):
        moved, block = trial_chunk(full_ref, curv_ref, lin_ref, lam_b, chunk, width)
        acc_ref[...] += lax.dot_general(
            moved.astype(BF), block, (((1,), (1,)), ((), ())), preferred_element_type=F32
        )
        return carry

    lax.fori_loop(0, COLS // width, step, 0)
    flat = acc_ref[0:1, :]
    return jnp.concatenate([flat[:, i * 128 : (i + 1) * 128] for i in range(NB)], axis=0)


def newton_update(lam, total, bound, hess_ref, inv_ref, scale):
    rhs = (total * (1.0 / NVAR) - bound) * scale
    step = times(inv_ref, rhs)
    for _ in range(2):
        step = step + times(inv_ref, rhs - times(hess_ref, step))
    return jnp.maximum(lam + step * scale, 0.0)


def gram_kernel(
    at_ref, own_hbm, one_hbm, two_hbm, three_hbm, curv_ref, lin_ref,
    full_ref, mine_ref, other_ref, top_ref, low_ref, prod_ref, half_ref, sems,
):
    quarter, core = at_ref[0], at_ref[1]
    start = pl.multiple_of(quarter * COLS, COLS)
    copies = [
        pltpu.make_async_copy(
            own_hbm.at[:, pl.ds(start, COLS)], full_ref.at[quarter], sems.at[0]
        )
    ]
    for k, piece in ((1, one_hbm), (2, two_hbm), (3, three_hbm)):
        copies.append(
            pltpu.make_async_copy(piece, full_ref.at[lax.rem(quarter + 4 - k, 4)], sems.at[k])
        )
    for copy in copies:
        copy.start()
    top_ref[...] = jnp.zeros_like(top_ref)
    low_ref[...] = jnp.zeros_like(low_ref)
    prod_ref[...] = jnp.zeros_like(prod_ref)
    for copy in copies:
        copy.wait()
    width = 1024
    count = width // 128
    nt = (((1,), (1,)), ((), ()))

    def step(chunk, carry):
        at = pl.multiple_of(chunk * width, width)
        block = full_ref[:, :, pl.ds(at, width)].reshape(M, width)
        curv = flat_rows(curv_ref, None, chunk * count, count)
        lin = flat_rows(lin_ref, None, chunk * count, count)
        weighted = (block.astype(F32) * curv).astype(BF)
        top_ref[...] += lax.dot_general(
            weighted[:256], block[:256], nt, preferred_element_type=F32
        )
        low_ref[...] += lax.dot_general(weighted[256:], block, nt, preferred_element_type=F32)
        moved = jnp.clip(-curv * lin, -move_limit, move_limit)
        moved = jnp.broadcast_to(moved, (16, width)).astype(BF)
        prod_ref[...] += lax.dot_general(moved, block, nt, preferred_element_type=F32)
        return carry

    lax.fori_loop(0, COLS // width, step, 0)
    for s in range(SHARDS):
        half_ref[s // HALF, s % HALF, SHARD_G:, :] = jnp.zeros((8, 128), F32)
    for j in range(NB):
        half_ref[0, j, SHARD_G : SHARD_G + 1, :] = prod_ref[0:1, j * 128 : (j + 1) * 128]
    for p, (i, j) in enumerate(PAIRS):
        for t in range(16):
            tile = p * 16 + t
            shard, row = tile // (SHARD_G // 8), tile % (SHARD_G // 8) * 8
            if i < 2:
                value = top_ref[i * 128 + t * 8 : i * 128 + t * 8 + 8, j * 128 : (j + 1) * 128]
            else:
                at = (i - 2) * 128 + t * 8
                value = low_ref[at : at + 8, j * 128 : (j + 1) * 128]
            half_ref[shard // HALF, shard % HALF, row : row + 8, :] = value
    mine_ref[...] = half_ref[core]
    other_ref[...] = half_ref[1 - core]


def split(value):
    high = value.astype(BF)
    return high, (value - high.astype(F32)).astype(BF)


def times_split(a_high, a_low, b_high, b_low):
    dot = functools.partial(jnp.dot, preferred_element_type=F32)
    return dot(a_high, b_high) + (dot(a_high, b_low) + dot(a_low, b_high))


def solve_kernel(
    at_ref, mine_ref, other_ref, full_ref, curv_ref, lin_ref, bound_ref,
    hess_ref, inv_ref, scale_ref, lam_ref, part_ref,
    half_ref, r_ref, prod_ref,
):
    core = at_ref[1]
    half_ref[core] = mine_ref[...]
    half_ref[1 - core] = other_ref[...]
    for p, (i, j) in enumerate(PAIRS):
        for t in range(16):
            tile = p * 16 + t
            shard, row = tile // (SHARD_G // 8), tile % (SHARD_G // 8) * 8
            hess_ref[i * 128 + t * 8 : i * 128 + t * 8 + 8, j * 128 : (j + 1) * 128] = (
                half_ref[shard // HALF, shard % HALF, row : row + 8, :] * (1.0 / NVAR)
            )
    row_id = lax.broadcasted_iota(jnp.int32, (128, 128), 0)
    col_id = lax.broadcasted_iota(jnp.int32, (128, 128), 1)
    diagonal = row_id == col_id
    for i in range(NB):
        at = slice(i * 128, (i + 1) * 128)
        for j in range(i):
            hess_ref[j * 128 : (j + 1) * 128, at] = hess_ref[at, j * 128 : (j + 1) * 128].T
        square = hess_ref[at, at]
        square = 0.5 * (square + square.T)
        hess_ref[at, at] = square
        values = jnp.sum(jnp.where(diagonal, square, 0.0), axis=0, keepdims=True)
        scale_ref[i : i + 1, :] = lax.rsqrt(values)
    scale = scale_ref[...]
    scale_row = jnp.concatenate([scale[i : i + 1, :] for i in range(NB)], axis=1)
    widest = jnp.zeros((1, M), F32)
    for i in range(NB):
        at = slice(i * 128, (i + 1) * 128)
        column = jnp.concatenate([down(scale[i : i + 1, :])] * NB, axis=1)
        rows = hess_ref[at, :] * column * scale_row
        hess_ref[at, :] = rows
        widest = widest + jnp.sum(jnp.abs(rows), axis=0, keepdims=True)
    alpha = 1.9 / jnp.max(widest)

    def eye():
        rid = lax.broadcasted_iota(jnp.int32, (M, M), 0)
        cid = lax.broadcasted_iota(jnp.int32, (M, M), 1)
        return (rid == cid).astype(F32)

    first = eye() - alpha * hess_ref[...]
    r_ref[...] = first
    inv_ref[...] = alpha * (eye() + first)

    def double(_, carry):
        r = r_ref[...].astype(BF)
        r2 = jnp.dot(r, r, preferred_element_type=F32)
        r_ref[...] = r2
        inv_ref[...] += jnp.dot(
            inv_ref[...].astype(BF), r2.astype(BF), preferred_element_type=F32
        )
        return carry

    lax.fori_loop(0, DOUBLINGS - 1, double, 0)

    def correct(state):
        count, _ = state
        x_high, x_low = split(inv_ref[...])
        h_high, h_low = split(hess_ref[...])
        residual = eye() - times_split(h_high, h_low, x_high, x_low)
        size = jnp.sum(residual * residual)
        good = size < M

        @pl.when(good)
        def _():
            r_high, r_low = split(residual)
            inv_ref[...] += times_split(x_high, x_low, r_high, r_low)

        @pl.when(jnp.logical_not(good))
        def _():
            inv_ref[...] = alpha * eye()

        return count + 1, size

    def unfinished(state):
        count, size = state
        return jnp.logical_and(jnp.logical_not(size < ACCEPT), count < MAX_CORRECT)

    _, size = lax.while_loop(unfinished, correct, (jnp.int32(0), jnp.float32(2.0 * M)))

    @pl.when(jnp.logical_not(size < ACCEPT))
    def _():
        inv_ref[...] = hess_ref[...]
        cid = lax.broadcasted_iota(jnp.int32, (8, M), 1)

        def pivot(k, carry):
            row = inv_ref[pl.ds(k, 1), :]
            here = lax.broadcasted_iota(jnp.int32, (1, M), 1) == k
            inverse = 1.0 / jnp.sum(jnp.where(here, row, 0.0))
            row = jnp.where(here, 1.0, row) * inverse

            def sweep(b, inner):
                at = pl.multiple_of(b * 8, 8)
                rows = inv_ref[pl.ds(at, 8), :]
                factor = jnp.sum(jnp.where(cid == k, rows, 0.0), axis=1, keepdims=True)
                rows = jnp.where(cid == k, 0.0, rows) - factor * row
                rid = lax.broadcasted_iota(jnp.int32, (8, M), 0) + at
                inv_ref[pl.ds(at, 8), :] = jnp.where(rid == k, row, rows)
                return inner

            lax.fori_loop(0, M // 8, sweep, 0)
            return carry

        lax.fori_loop(0, M, pivot, 0)

    total = jnp.concatenate(
        [half_ref[0, j, SHARD_G : SHARD_G + 1, :] for j in range(NB)], axis=0
    )
    zero = jnp.zeros((NB, 128), F32)
    lam = newton_update(zero, total, bound_ref[...], hess_ref, inv_ref, scale)
    lam_ref[...] = lam
    part_ref[...] = product_of_trial(full_ref, curv_ref, lin_ref, lam, prod_ref)


def step_kernel(
    gathered_ref, lam_in_ref, full_ref, curv_ref, lin_ref, bound_ref, hess_ref, inv_ref, scale_ref,
    lam_ref, part_ref, prod_ref,
):
    total = jnp.sum(gathered_ref[...], axis=0)
    lam = newton_update(
        lam_in_ref[...], total, bound_ref[...], hess_ref, inv_ref, scale_ref[...]
    )
    lam_ref[...] = lam
    part_ref[...] = product_of_trial(full_ref, curv_ref, lin_ref, lam, prod_ref)


def last_kernel(
    gathered_ref, lam_in_ref, full_ref, curv_ref, lin_ref, bound_ref, hess_ref, inv_ref, scale_ref,
    lam_ref, step_ref,
):
    total = jnp.sum(gathered_ref[...], axis=0)
    lam = newton_update(
        lam_in_ref[...], total, bound_ref[...], hess_ref, inv_ref, scale_ref[...]
    )
    lam_ref[...] = lam
    lam_b = as_rows(lam)
    width = 1024
    for chunk in range(COLS // width):
        moved, _ = trial_chunk(full_ref, curv_ref, lin_ref, lam_b, chunk, width)
        for k in range(width // 128):
            step_ref[chunk * (width // 128) + k : chunk * (width // 128) + k + 1, :] = moved[
                0:1, k * 128 : (k + 1) * 128
            ]


VM = pl.BlockSpec(memory_space=pltpu.VMEM)
SM = pl.BlockSpec(memory_space=pltpu.SMEM)
ANY = pl.BlockSpec(memory_space=pl.ANY)


def sds(shape, dtype=F32):
    return jax.ShapeDtypeStruct(shape, dtype)


def call(kernel, ins, outs, scratch, mib, name):
    return pl.pallas_call(
        kernel,
        in_specs=ins,
        out_specs=[VM] * len(outs),
        out_shape=outs,
        scratch_shapes=scratch,
        compiler_params=pltpu.CompilerParams(vmem_limit_bytes=mib * MIB),
        name=name,
    )


def summed(part):
    near = from_everyone(part, NEAR).sum(axis=0)
    return from_everyone(near, FAR)


def on_device(gradients, perm, weights, linear, bound):
    here = lax.axis_index(BRICK)
    quarter = lax.axis_index("grp")
    core = lax.axis_index("brick_2")
    per_brick = gradients.shape[1] // 128
    at = jnp.stack([quarter, core]).astype(jnp.int32)

    def toward(k):
        to = lax.rem(quarter + k, 4) * COLS
        piece = lax.dynamic_slice(gradients, (0, to), (ROWS, COLS))
        return lax.ppermute(piece, "grp", [(i, (i + k) % 4) for i in range(4)])

    two, one, three = toward(2), toward(1), toward(3)

    outgoing, arrival, place = layout_tables(perm, here, per_brick)
    inverse = lax.dynamic_slice_in_dim(jnp.argsort(outgoing), quarter * BLKS, BLKS)
    both = jnp.concatenate([weights.reshape(BLKS, 128), linear.reshape(BLKS, 128)], axis=1)
    both = from_everyone(both, "grp").reshape(per_brick, 256)
    back = lax.all_to_all(both[arrival], BRICK, 0, 0, tiled=True)[inverse]
    curv, lin = back[:, :128], back[:, 128:]

    packed = (HALF, SHARD, 128)
    full, mine, other = call(
        gram_kernel,
        [SM, ANY, ANY, ANY, ANY, VM, VM],
        [sds((NB, ROWS, COLS), BF), sds(packed), sds(packed)],
        [
            pltpu.VMEM((256, 256), F32),
            pltpu.VMEM((256, 512), F32),
            pltpu.VMEM((16, M), F32),
            pltpu.VMEM((2, *packed), F32),
            pltpu.SemaphoreType.DMA((4,)),
        ],
        24,
        "gram",
    )(at, gradients, one, two, three, curv, lin)

    swap = [(0, 1), (1, 0)]
    mine = mine + lax.ppermute(other, "brick_2", swap)
    shard = lax.all_to_all(mine, PLANE, 0, 0, tiled=True).sum(axis=0)
    shard = from_everyone(shard, "brick_1").sum(axis=0)
    mine = from_everyone(shard, PLANE)
    other = lax.ppermute(mine, "brick_2", swap)

    bound = bound.reshape(NB, 128)
    square = sds((M, M))
    vector = sds((NB, 128))
    hess, inv, scale, lam, part = call(
        solve_kernel,
        [SM, VM, VM, VM, VM, VM, VM],
        [square, square, vector, vector, vector],
        [pltpu.VMEM((2, *packed), F32), pltpu.VMEM((M, M), F32), pltpu.VMEM((16, M), F32)],
        32,
        "solve",
    )(at, mine, other, full, curv, lin, bound)
    for _ in range(ITERS - 2):
        lam, part = call(
            step_kernel, [VM] * 9, [vector, vector], [pltpu.VMEM((16, M), F32)], 24, "step"
        )(summed(part), lam, full, curv, lin, bound, hess, inv, scale)
    lam, result = call(
        last_kernel, [VM] * 9, [vector, sds((BLKS, 128))], [], 24, "last"
    )(summed(part), lam, full, curv, lin, bound, hess, inv, scale)

    whole = from_everyone(result, "grp").reshape(per_brick, 128)
    arrived = lax.all_to_all(whole[outgoing], BRICK, 0, 0, tiled=True)
    place = lax.dynamic_slice_in_dim(place, quarter * BLKS, BLKS)
    return (arrived[place].reshape(-1), lam.reshape(-1))


def solution(mesh):
    torus = Mesh(
        mesh.devices.reshape(4, 8, 2, mesh.shape["grp"]), ("brick_0", "brick_1", "brick_2", "grp")
    )
    placed = (P("grp", BRICK), P(), P(BRICK_GRP), P(BRICK_GRP), P())
    return jax.shard_map(
        on_device, mesh=torus, in_specs=placed, out_specs=(P(BRICK_GRP), P()), check_vma=False
    )
```

```python
import functools

import jax
import jax.numpy as jnp
from jax import lax
from jax.experimental import pallas as pl
from jax.experimental.pallas import tpu as pltpu
from jax.sharding import Mesh
from jax.sharding import PartitionSpec as P

ITERS = 4
BRICK = ("brick_0", "brick_1", "brick_2")
BRICK_GRP = ("brick_0", "brick_1", "brick_2", "grp")
FAR = ("brick_0", "brick_1")
NEAR = ("brick_2", "grp")
PLANE = ("brick_0", "grp")
M = 512
ROWS = 128
NB = M // ROWS
COLS = 4096
BLKS = COLS // 128
NVAR = 1048576
PAIRS = [(i, j) for i in range(NB) for j in range(i + 1)]
SHARDS = 32
SHARD_G = len(PAIRS) * ROWS // SHARDS
SHARD = SHARD_G + 8
HALF = SHARDS // 2
DOUBLINGS = 5
MAX_CORRECT = 48
ACCEPT = 1e-4

move_limit = 1.0
MIB = 1024 * 1024
BF = jnp.bfloat16
F32 = jnp.float32


def size_of(axis):
    return lax.axis_size(axis)


def from_everyone(array, axis):
    devices = size_of(axis)
    return lax.all_to_all(
        jnp.broadcast_to(array[None], (devices, *array.shape)), axis, 0, 0, tiled=True
    )


def first_of(mask, values, count):
    index = lax.broadcasted_iota(jnp.int32, values.shape, 1)
    _, kept = lax.sort_key_val(jnp.where(mask, index, index + values.shape[1]), values)
    return kept[:, :count]


def ranks(keys):
    return jnp.sum(keys[None, :] < keys[:, None], axis=1, dtype=jnp.int32)


def inverted(places, count):
    slots = jnp.arange(count, dtype=jnp.int32)
    index = jnp.arange(places.shape[0], dtype=jnp.int32)
    return jnp.sum(jnp.where(places[None, :] == slots[:, None], index[None, :], 0), axis=1)


def layout_tables(perm, here, per_brick):
    chip, core = here // 2, here % 2
    per_chip = 2 * per_brick
    grid = perm.reshape(-1, per_brick)
    incoming = first_of(grid // per_brick == here, grid, 2).reshape(-1) % per_brick
    local = lax.dynamic_slice_in_dim(perm, chip * per_chip, per_chip)
    index = jnp.arange(per_chip, dtype=jnp.int32)
    key = (local // per_chip) * per_chip + index
    key = jnp.where((local // per_brick) % 2 == core, key, key + perm.shape[0] * 2)
    leaving = inverted(ranks(key), per_brick)
    same = lax.dynamic_index_in_dim(grid.reshape(-1, 2, per_brick), core, 1, keepdims=False)
    back = first_of(same // per_chip == chip, same, 4).reshape(-1) % per_chip
    mine = lax.dynamic_slice_in_dim(perm, here * per_brick, per_brick)
    place = ranks((mine // per_chip) * per_brick + jnp.arange(per_brick, dtype=jnp.int32))
    return (inverted(incoming, per_brick), leaving, back, place)


def down(row):
    return jnp.broadcast_to(row, (128, 128)).T


def times(mat_ref, vec):
    total = [jnp.zeros((8, 128), F32) for _ in range(NB)]
    for i in range(NB):
        column = down(vec[i : i + 1, :])
        for j in range(NB):
            part = mat_ref[i * 128 : (i + 1) * 128, j * 128 : (j + 1) * 128] * column
            total[j] = total[j] + part.reshape(16, 8, 128).sum(axis=0)
    return jnp.concatenate([t.sum(axis=0, keepdims=True) for t in total], axis=0)


WIDTH = 1024
CHUNKS = COLS // WIDTH
NT = (((1,), (1,)), ((), ()))


def flat_rows(ref, chunk):
    count = WIDTH // 128
    rows = [ref[chunk * count + k : chunk * count + k + 1, :] for k in range(count)]
    return jnp.concatenate(rows, axis=1)


class Columns:
    def __init__(self, at_ref, pieces, full_ref, sems):
        quarter = at_ref[0]
        self.full_ref = full_ref
        self.copies = []
        for chunk in range(CHUNKS):
            to = pl.ds(chunk * WIDTH, WIDTH)
            own = pl.ds(pl.multiple_of(quarter * COLS + chunk * WIDTH, WIDTH), WIDTH)
            self.copies.append(
                [
                    pltpu.make_async_copy(
                        piece.at[:, own if k == 0 else to],
                        full_ref.at[lax.rem(quarter + 4 - k, 4), :, to],
                        sems.at[chunk, k],
                    )
                    for k, piece in enumerate(pieces)
                ]
            )

    def start(self):
        for group in self.copies:
            for copy in group:
                copy.start()

    def chunk(self, chunk):
        for copy in self.copies[chunk]:
            copy.wait()
        return self.full_ref[:, :, chunk * WIDTH : (chunk + 1) * WIDTH].reshape(M, WIDTH)


def as_rows(lam):
    flat = jnp.concatenate([lam[i : i + 1, :] for i in range(NB)], axis=1)
    return jnp.broadcast_to(flat, (16, M)).astype(BF)


def as_lines(flat):
    return jnp.concatenate([flat[:, i * 128 : (i + 1) * 128] for i in range(NB)], axis=0)


def trial_chunk(block, curv_ref, lin_ref, lam_b, chunk):
    pushed = jnp.dot(lam_b, block, preferred_element_type=F32)
    curv, lin = flat_rows(curv_ref, chunk), flat_rows(lin_ref, chunk)
    return jnp.clip(-curv * (lin + pushed), -move_limit, move_limit)


def product_of_trial(columns, curv_ref, lin_ref, lam):
    lam_b = as_rows(lam)
    total = jnp.zeros((16, M), F32)
    for chunk in range(CHUNKS):
        block = columns.chunk(chunk)
        moved = trial_chunk(block, curv_ref, lin_ref, lam_b, chunk).astype(BF)
        total += lax.dot_general(moved, block, NT, preferred_element_type=F32)
    return as_lines(total[0:1, :])


def newton_update(lam, total, bound, inv_ref, scale):
    rhs = (total * (1.0 / NVAR) - bound) * scale
    return jnp.maximum(lam + times(inv_ref, rhs) * scale, 0.0)


def packed_tile(p, t):
    tile = p * 16 + t
    shard, row = tile // (SHARD_G // 8), tile % (SHARD_G // 8) * 8
    return shard // HALF, shard % HALF, slice(row, row + 8)


def gram_kernel(
    at_ref, own_hbm, one_hbm, two_hbm, three_hbm, curv_ref, lin_ref,
    mine_ref, other_ref, full_ref, gram_ref, prod_ref, half_ref, sems,
):
    core = at_ref[1]
    columns = Columns(at_ref, (own_hbm, one_hbm, two_hbm, three_hbm), full_ref, sems)
    columns.start()
    gram_ref[...] = jnp.zeros_like(gram_ref)
    prod_ref[...] = jnp.zeros_like(prod_ref)
    for s in range(SHARDS):
        half_ref[s // HALF, s % HALF, SHARD_G:, :] = jnp.zeros((8, 128), F32)
    for chunk in range(CHUNKS):
        block = columns.chunk(chunk)
        curv, lin = flat_rows(curv_ref, chunk), flat_rows(lin_ref, chunk)
        weighted = (block.astype(F32) * curv).astype(BF)
        gram_ref[...] += lax.dot_general(weighted, block, NT, preferred_element_type=F32)
        moved = jnp.clip(-curv * lin, -move_limit, move_limit)
        moved = jnp.broadcast_to(moved, (16, WIDTH)).astype(BF)
        prod_ref[...] += lax.dot_general(moved, block, NT, preferred_element_type=F32)
    for j in range(NB):
        half_ref[0, j, SHARD_G : SHARD_G + 1, :] = prod_ref[0:1, j * 128 : (j + 1) * 128]
    for p, (i, j) in enumerate(PAIRS):
        rows, cols = slice(i * 128, (i + 1) * 128), slice(j * 128, (j + 1) * 128)
        value = 0.5 * (gram_ref[rows, cols] + gram_ref[cols, rows].T)
        for t in range(16):
            half_ref[packed_tile(p, t)] = value[t * 8 : t * 8 + 8]
    mine_ref[...] = half_ref[core]
    other_ref[...] = half_ref[1 - core]


def split(value):
    high = value.astype(BF)
    return high, (value - high.astype(F32)).astype(BF)


def times_split(a_high, a_low, b_high, b_low):
    dot = functools.partial(jnp.dot, preferred_element_type=F32)
    return dot(a_high, b_high) + (dot(a_high, b_low) + dot(a_low, b_high))


def solve_kernel(
    at_ref, own_hbm, one_hbm, two_hbm, three_hbm, mine_ref, other_ref, curv_ref, lin_ref, bound_ref,
    inv_ref, scale_ref, lam_ref, part_ref,
    full_ref, half_ref, hess_ref, r_ref, sems,
):
    columns = Columns(at_ref, (own_hbm, one_hbm, two_hbm, three_hbm), full_ref, sems)
    columns.start()
    core = at_ref[1]
    half_ref[core] = mine_ref[...]
    half_ref[1 - core] = other_ref[...]
    for p, (i, j) in enumerate(PAIRS):
        for t in range(16):
            at = i * 128 + t * 8
            hess_ref[at : at + 8, j * 128 : (j + 1) * 128] = half_ref[packed_tile(p, t)] * (
                1.0 / NVAR
            )
    row_id = lax.broadcasted_iota(jnp.int32, (128, 128), 0)
    col_id = lax.broadcasted_iota(jnp.int32, (128, 128), 1)
    diagonal = row_id == col_id
    for i in range(NB):
        at = slice(i * 128, (i + 1) * 128)
        for j in range(i):
            hess_ref[j * 128 : (j + 1) * 128, at] = hess_ref[at, j * 128 : (j + 1) * 128].T
        values = jnp.sum(jnp.where(diagonal, hess_ref[at, at], 0.0), axis=0, keepdims=True)
        scale_ref[i : i + 1, :] = lax.rsqrt(values)
    scale = scale_ref[...]
    scale_row = jnp.concatenate([scale[i : i + 1, :] for i in range(NB)], axis=1)
    widest = jnp.zeros((1, M), F32)
    for i in range(NB):
        at = slice(i * 128, (i + 1) * 128)
        column = jnp.concatenate([down(scale[i : i + 1, :])] * NB, axis=1)
        rows = hess_ref[at, :] * column * scale_row
        hess_ref[at, :] = rows
        widest = widest + jnp.sum(jnp.abs(rows), axis=0, keepdims=True)
    alpha = 1.9 / jnp.max(widest)

    def eye():
        rid = lax.broadcasted_iota(jnp.int32, (M, M), 0)
        cid = lax.broadcasted_iota(jnp.int32, (M, M), 1)
        return (rid == cid).astype(F32)

    first = eye() - alpha * hess_ref[...]
    r_ref[...] = first
    inv_ref[...] = alpha * (eye() + first)

    def double(_, carry):
        r = r_ref[...].astype(BF)
        r2 = jnp.dot(r, r, preferred_element_type=F32)
        r_ref[...] = r2
        inv_ref[...] += jnp.dot(
            inv_ref[...].astype(BF), r2.astype(BF), preferred_element_type=F32
        )
        return carry

    lax.fori_loop(0, DOUBLINGS - 1, double, 0)

    def correct(precise):
        x = inv_ref[...]
        x_high, x_low = split(x)
        if precise:
            product = jnp.dot(
                hess_ref[...], x, precision=lax.Precision.HIGHEST, preferred_element_type=F32
            )
        else:
            h_high, h_low = split(hess_ref[...])
            product = times_split(h_high, h_low, x_high, x_low)
        residual = eye() - product
        size = jnp.sum(residual * residual)
        good = size < M

        @pl.when(good)
        def _():
            r_high, r_low = split(residual)
            inv_ref[...] += times_split(x_high, x_low, r_high, r_low)

        @pl.when(jnp.logical_not(good))
        def _():
            inv_ref[...] = alpha * eye()

        return size

    def correct_again(state):
        return state[0] + 1, correct(True)

    def unfinished(state):
        count, size = state
        return jnp.logical_and(jnp.logical_not(size < ACCEPT), count < MAX_CORRECT)

    correct(False)
    _, size = lax.while_loop(unfinished, correct_again, (jnp.int32(0), jnp.float32(2.0 * M)))

    @pl.when(jnp.logical_not(size < ACCEPT))
    def _():
        inv_ref[...] = hess_ref[...]
        cid = lax.broadcasted_iota(jnp.int32, (8, M), 1)

        def pivot(k, carry):
            row = inv_ref[pl.ds(k, 1), :]
            here = lax.broadcasted_iota(jnp.int32, (1, M), 1) == k
            inverse = 1.0 / jnp.sum(jnp.where(here, row, 0.0))
            row = jnp.where(here, 1.0, row) * inverse

            def sweep(b, inner):
                at = pl.multiple_of(b * 8, 8)
                rows = inv_ref[pl.ds(at, 8), :]
                factor = jnp.sum(jnp.where(cid == k, rows, 0.0), axis=1, keepdims=True)
                rows = jnp.where(cid == k, 0.0, rows) - factor * row
                rid = lax.broadcasted_iota(jnp.int32, (8, M), 0) + at
                inv_ref[pl.ds(at, 8), :] = jnp.where(rid == k, row, rows)
                return inner

            lax.fori_loop(0, M // 8, sweep, 0)
            return carry

        lax.fori_loop(0, M, pivot, 0)

    total = jnp.concatenate(
        [half_ref[0, j, SHARD_G : SHARD_G + 1, :] for j in range(NB)], axis=0
    )
    zero = jnp.zeros((NB, 128), F32)
    lam = newton_update(zero, total, bound_ref[...], inv_ref, scale)
    lam_ref[...] = lam
    part_ref[...] = product_of_trial(columns, curv_ref, lin_ref, lam)


def updated(gathered_ref, lam_in_ref, bound_ref, inv_hbm, scale_ref, inv_ref, inv_sem):
    copy = pltpu.make_async_copy(inv_hbm, inv_ref, inv_sem)
    copy.start()
    return lambda: (
        copy.wait(),
        newton_update(
            lam_in_ref[...],
            jnp.sum(gathered_ref[...], axis=0),
            bound_ref[...],
            inv_ref,
            scale_ref[...],
        ),
    )[1]


def step_kernel(
    at_ref, own_hbm, one_hbm, two_hbm, three_hbm, inv_hbm,
    gathered_ref, lam_in_ref, curv_ref, lin_ref, bound_ref, scale_ref,
    lam_ref, part_ref, full_ref, inv_ref, sems, inv_sem,
):
    update = updated(gathered_ref, lam_in_ref, bound_ref, inv_hbm, scale_ref, inv_ref, inv_sem)
    columns = Columns(at_ref, (own_hbm, one_hbm, two_hbm, three_hbm), full_ref, sems)
    columns.start()
    lam = update()
    lam_ref[...] = lam
    part_ref[...] = product_of_trial(columns, curv_ref, lin_ref, lam)


def last_kernel(
    at_ref, own_hbm, one_hbm, two_hbm, three_hbm, inv_hbm,
    gathered_ref, lam_in_ref, curv_ref, lin_ref, bound_ref, scale_ref,
    lam_ref, step_ref, full_ref, inv_ref, sems, inv_sem,
):
    update = updated(gathered_ref, lam_in_ref, bound_ref, inv_hbm, scale_ref, inv_ref, inv_sem)
    columns = Columns(at_ref, (own_hbm, one_hbm, two_hbm, three_hbm), full_ref, sems)
    columns.start()
    lam = update()
    lam_ref[...] = lam
    lam_b = as_rows(lam)
    count = WIDTH // 128
    for chunk in range(CHUNKS):
        moved = trial_chunk(columns.chunk(chunk), curv_ref, lin_ref, lam_b, chunk)
        for k in range(count):
            at = chunk * count + k
            step_ref[at : at + 1, :] = moved[0:1, k * 128 : (k + 1) * 128]


VM = pl.BlockSpec(memory_space=pltpu.VMEM)
SM = pl.BlockSpec(memory_space=pltpu.SMEM)
ANY = pl.BlockSpec(memory_space=pl.ANY)


def sds(shape, dtype=F32):
    return jax.ShapeDtypeStruct(shape, dtype)


def call(kernel, ins, outs, scratch, mib, name):
    return pl.pallas_call(
        kernel,
        in_specs=ins,
        out_specs=[VM] * len(outs),
        out_shape=outs,
        scratch_shapes=scratch,
        compiler_params=pltpu.CompilerParams(vmem_limit_bytes=mib * MIB),
        name=name,
    )


def summed(part):
    near = from_everyone(part, NEAR).sum(axis=0)
    return from_everyone(near, FAR)


def on_device(gradients, perm, weights, linear, bound):
    here = lax.axis_index(BRICK)
    quarter = lax.axis_index("grp")
    core = lax.axis_index("brick_2")
    per_brick = gradients.shape[1] // 128
    at = jnp.stack([quarter, core]).astype(jnp.int32)

    both = jnp.concatenate([weights.reshape(BLKS, 128), linear.reshape(BLKS, 128)], axis=1)
    both = from_everyone(both, NEAR)

    slices = [
        lax.dynamic_slice(gradients, (0, lax.rem(quarter + k, 4) * COLS), (ROWS, COLS))
        for k in (1, 2, 3)
    ]
    *slices, both = lax.optimization_barrier((*slices, both))
    one, two, three = [
        lax.ppermute(piece, "grp", [(i, (i + k + 1) % 4) for i in range(4)])
        for k, piece in enumerate(slices)
    ]
    pieces = (gradients, one, two, three)

    incoming, leaving, back, place = layout_tables(perm, here, per_brick)
    incoming = lax.dynamic_slice_in_dim(incoming, quarter * BLKS, BLKS)
    place = lax.dynamic_slice_in_dim(place, quarter * BLKS, BLKS)
    both = lax.all_to_all(both.reshape(-1, 256)[leaving], FAR, 0, 0, tiled=True)[incoming]
    curv, lin, back, place = lax.optimization_barrier((both[:, :128], both[:, 128:], back, place))

    packed = (HALF, SHARD, 128)
    full = pltpu.VMEM((NB, ROWS, COLS), BF)
    sems = pltpu.SemaphoreType.DMA((CHUNKS, NB))
    mine, other = call(
        gram_kernel,
        [SM, ANY, ANY, ANY, ANY, VM, VM],
        [sds(packed), sds(packed)],
        [
            full,
            pltpu.VMEM((M, M), F32),
            pltpu.VMEM((16, M), F32),
            pltpu.VMEM((2, *packed), F32),
            sems,
        ],
        24,
        "gram",
    )(at, *pieces, curv, lin)

    swap = [(0, 1), (1, 0)]
    mine = mine + lax.ppermute(other, "brick_2", swap)
    shard = lax.all_to_all(mine, PLANE, 0, 0, tiled=True).sum(axis=0)
    shard = from_everyone(shard, "brick_1").sum(axis=0)
    mine = from_everyone(shard, PLANE)
    other = lax.ppermute(mine, "brick_2", swap)

    bound = bound.reshape(NB, 128)
    square = sds((M, M))
    vector = sds((NB, 128))
    inv, scale, lam, part = call(
        solve_kernel,
        [SM, ANY, ANY, ANY, ANY, VM, VM, VM, VM, VM],
        [square, vector, vector, vector],
        [
            full,
            pltpu.VMEM((2, *packed), F32),
            pltpu.VMEM((M, M), F32),
            pltpu.VMEM((M, M), F32),
            sems,
        ],
        32,
        "solve",
    )(at, *pieces, mine, other, curv, lin, bound)
    ins = [SM, ANY, ANY, ANY, ANY, ANY, VM, VM, VM, VM, VM, VM]
    scratch = [full, pltpu.VMEM((M, M), F32), sems, pltpu.SemaphoreType.DMA(())]
    for _ in range(ITERS - 2):
        lam, part = call(step_kernel, ins, [vector, vector], scratch, 24, "step")(
            at, *pieces, inv, summed(part), lam, curv, lin, bound, scale
        )
    lam, result = call(last_kernel, ins, [vector, sds((BLKS, 128))], scratch, 24, "last")(
        at, *pieces, inv, summed(part), lam, curv, lin, bound, scale
    )

    whole = from_everyone(result, NEAR).reshape(-1, 128)
    arrived = lax.all_to_all(whole[back], FAR, 0, 0, tiled=True)
    return (arrived[place].reshape(-1), lam.reshape(-1))


def solution(mesh):
    torus = Mesh(
        mesh.devices.reshape(4, 8, 2, mesh.shape["grp"]), ("brick_0", "brick_1", "brick_2", "grp")
    )
    placed = (P("grp", BRICK), P(), P(BRICK_GRP), P(BRICK_GRP), P())
    return jax.shard_map(
        on_device, mesh=torus, in_specs=placed, out_specs=(P(BRICK_GRP), P()), check_vma=False
    )
```

```python
import functools

import jax
import jax.numpy as jnp
from jax import lax
from jax.experimental import pallas as pl
from jax.experimental.pallas import tpu as pltpu
from jax.sharding import Mesh
from jax.sharding import PartitionSpec as P


ITERS = 4
BRICK = ("brick_0", "brick_1", "brick_2")
BRICK_GRP = ("brick_0", "brick_1", "brick_2", "grp")
FAR = ("brick_0", "brick_1")
NEAR = ("brick_2", "grp")
PLANE = ("brick_0", "grp")
M = 512
ROWS = 128
NB = M // ROWS
COLS = 4096
BLKS = COLS // 128
NVAR = 1048576
PAIRS = [(i, j) for i in range(NB) for j in range(i + 1)]
SHARDS = 32
SHARD_G = len(PAIRS) * ROWS // SHARDS
SHARD = SHARD_G + 8
HALF = SHARDS // 2
DOUBLINGS = 4
MAX_CORRECT = 48
ACCEPT = 1e-4

move_limit = 1.0
MIB = 1024 * 1024
BF = jnp.bfloat16
F32 = jnp.float32


def size_of(axis):
    return lax.axis_size(axis)


def from_everyone(array, axis):
    devices = size_of(axis)
    return lax.all_to_all(
        jnp.broadcast_to(array[None], (devices, *array.shape)), axis, 0, 0, tiled=True
    )


def two_of(mask, values):
    index = lax.broadcasted_iota(jnp.int32, values.shape, 1)
    first = jnp.min(jnp.where(mask, index, values.shape[1]), axis=1, keepdims=True)
    second = jnp.max(jnp.where(mask, index, -1), axis=1, keepdims=True)
    kept = [jnp.sum(jnp.where(index == at, values, 0), axis=1) for at in (first, second)]
    return jnp.stack(kept, axis=1)


def ranks(keys):
    return jnp.sum(keys[None, :] < keys[:, None], axis=1, dtype=jnp.int32)


def inverted(places, count):
    slots = jnp.arange(count, dtype=jnp.int32)
    index = jnp.arange(places.shape[0], dtype=jnp.int32)
    return jnp.sum(jnp.where(places[None, :] == slots[:, None], index[None, :], 0), axis=1)


def layout_tables(perm, here, per_brick):
    chip, core = here // 2, here % 2
    per_chip = 2 * per_brick
    grid = perm.reshape(-1, per_brick)
    same = lax.dynamic_index_in_dim(grid.reshape(-1, 2, per_brick), core, 1, keepdims=False)
    rows = jnp.concatenate([grid, same, same], axis=0)
    bricks, chips = grid.shape[0], same.shape[0]
    line = lax.broadcasted_iota(jnp.int32, rows.shape, 0)
    wanted = jnp.where(line < bricks, here, chip * 2 + (line >= bricks + chips))
    picked = two_of(rows // per_brick == wanted, rows)
    incoming = picked[:bricks].reshape(-1) % per_brick
    back = jnp.stack([picked[bricks : bricks + chips], picked[bricks + chips :]], axis=1)
    back = back.reshape(-1) % per_chip
    local = lax.dynamic_slice_in_dim(perm, chip * per_chip, per_chip)
    index = jnp.arange(per_chip, dtype=jnp.int32)
    key = (local // per_chip) * per_chip + index
    key = jnp.where((local // per_brick) % 2 == core, key, key + perm.shape[0] * 2)
    leaving = inverted(ranks(key), per_brick)
    mine = lax.dynamic_slice_in_dim(perm, here * per_brick, per_brick)
    place = ranks((mine // per_brick) * per_brick + jnp.arange(per_brick, dtype=jnp.int32))
    return (inverted(incoming, per_brick), leaving, back, place)


def down(row):
    return jnp.broadcast_to(row, (128, 128)).T


def times(mat_ref, vec):
    total = [jnp.zeros((8, 128), F32) for _ in range(NB)]
    for i in range(NB):
        column = down(vec[i : i + 1, :])
        for j in range(NB):
            part = mat_ref[i * 128 : (i + 1) * 128, j * 128 : (j + 1) * 128] * column
            total[j] = total[j] + part.reshape(16, 8, 128).sum(axis=0)
    return jnp.concatenate([t.sum(axis=0, keepdims=True) for t in total], axis=0)


WIDTH = 1024
CHUNKS = COLS // WIDTH
NT = (((1,), (1,)), ((), ()))


def flat_rows(ref, chunk):
    count = WIDTH // 128
    rows = [ref[chunk * count + k : chunk * count + k + 1, :] for k in range(count)]
    return jnp.concatenate(rows, axis=1)


def columns(pieces, chunk):
    to = slice(chunk * WIDTH, (chunk + 1) * WIDTH)
    return jnp.concatenate([piece[:, to] for piece in pieces], axis=0)


def slots(at_ref):
    return [lax.rem(at_ref[0] + NB - k, NB) for k in range(NB)]


def as_rows(at_ref, lam_ref):
    flat = jnp.concatenate([lam_ref[pl.ds(slot, 1), :] for slot in slots(at_ref)], axis=1)
    return jnp.broadcast_to(flat, (16, M)).astype(BF)


def trial_chunk(block, curv_ref, lin_ref, lam_b, chunk):
    pushed = jnp.dot(lam_b, block, preferred_element_type=F32)
    curv, lin = flat_rows(curv_ref, chunk), flat_rows(lin_ref, chunk)
    return jnp.clip(-curv * (lin + pushed), -move_limit, move_limit)


def product_of_trial(at_ref, pieces, curv_ref, lin_ref, lam_ref, part_ref):
    lam_b = as_rows(at_ref, lam_ref)
    total = jnp.zeros((16, M), F32)
    for chunk in range(CHUNKS):
        block = columns(pieces, chunk)
        moved = trial_chunk(block, curv_ref, lin_ref, lam_b, chunk).astype(BF)
        total += lax.dot_general(moved, block, NT, preferred_element_type=F32)
    for k, slot in enumerate(slots(at_ref)):
        part_ref[pl.ds(slot, 1), :] = total[0:1, k * 128 : (k + 1) * 128]


def newton_update(lam, total, bound, inv_ref, scale):
    rhs = (total * (1.0 / NVAR) - bound) * scale
    return jnp.maximum(lam + times(inv_ref, rhs) * scale, 0.0)


def packed_tile(p, t):
    tile = p * 16 + t
    shard, row = tile // (SHARD_G // 8), tile % (SHARD_G // 8) * 8
    return shard // HALF, shard % HALF, slice(row, row + 8)


def gram_kernel(
    at_ref, own_ref, one_ref, two_ref, three_ref, curv_ref, lin_ref,
    mine_ref, other_ref, gram_ref, prod_ref, block_ref, half_ref,
):
    core = at_ref[1]
    pieces = (own_ref, one_ref, two_ref, three_ref)
    gram_ref[...] = jnp.zeros_like(gram_ref)
    prod_ref[...] = jnp.zeros_like(prod_ref)
    for s in range(SHARDS):
        half_ref[s // HALF, s % HALF, SHARD_G:, :] = jnp.zeros((8, 128), F32)
    for chunk in range(CHUNKS):
        block = columns(pieces, chunk)
        curv, lin = flat_rows(curv_ref, chunk), flat_rows(lin_ref, chunk)
        weighted = (block.astype(F32) * curv).astype(BF)
        gram_ref[...] += lax.dot_general(weighted, block, NT, preferred_element_type=F32)
        moved = jnp.clip(-curv * lin, -move_limit, move_limit)
        moved = jnp.broadcast_to(moved, (16, WIDTH)).astype(BF)
        prod_ref[...] += lax.dot_general(moved, block, NT, preferred_element_type=F32)
    where = slots(at_ref)
    for a in range(NB):
        half_ref[0, pl.ds(where[a], 1), SHARD_G, :] = prod_ref[0:1, a * 128 : (a + 1) * 128]
        for b in range(NB):
            block_ref[where[a], where[b]] = gram_ref[
                a * 128 : (a + 1) * 128, b * 128 : (b + 1) * 128
            ]
    for p, (i, j) in enumerate(PAIRS):
        value = 0.5 * (block_ref[i, j] + block_ref[j, i].T)
        for t in range(16):
            half_ref[packed_tile(p, t)] = value[t * 8 : t * 8 + 8]
    mine_ref[...] = half_ref[core]
    other_ref[...] = half_ref[1 - core]


def split(value):
    high = value.astype(BF)
    return high, (value - high.astype(F32)).astype(BF)


def times_split(a_high, a_low, b_high, b_low):
    dot = functools.partial(jnp.dot, preferred_element_type=F32)
    return dot(a_high, b_high) + (dot(a_high, b_low) + dot(a_low, b_high))


def solve_kernel(
    at_ref, own_ref, one_ref, two_ref, three_ref, mine_ref, other_ref, curv_ref, lin_ref, bound_ref,
    inv_ref, scale_ref, lam_ref, part_ref,
    half_ref, hess_ref, r_ref,
):
    pieces = (own_ref, one_ref, two_ref, three_ref)
    core = at_ref[1]
    half_ref[core] = mine_ref[...]
    half_ref[1 - core] = other_ref[...]
    for p, (i, j) in enumerate(PAIRS):
        for t in range(16):
            at = i * 128 + t * 8
            hess_ref[at : at + 8, j * 128 : (j + 1) * 128] = half_ref[packed_tile(p, t)] * (
                1.0 / NVAR
            )
    row_id = lax.broadcasted_iota(jnp.int32, (128, 128), 0)
    col_id = lax.broadcasted_iota(jnp.int32, (128, 128), 1)
    diagonal = row_id == col_id
    for i in range(NB):
        at = slice(i * 128, (i + 1) * 128)
        for j in range(i):
            hess_ref[j * 128 : (j + 1) * 128, at] = hess_ref[at, j * 128 : (j + 1) * 128].T
        values = jnp.sum(jnp.where(diagonal, hess_ref[at, at], 0.0), axis=0, keepdims=True)
        scale_ref[i : i + 1, :] = lax.rsqrt(values)
    scale = scale_ref[...]
    scale_row = jnp.concatenate([scale[i : i + 1, :] for i in range(NB)], axis=1)
    widest = jnp.zeros((1, M), F32)
    for i in range(NB):
        at = slice(i * 128, (i + 1) * 128)
        column = jnp.concatenate([down(scale[i : i + 1, :])] * NB, axis=1)
        rows = hess_ref[at, :] * column * scale_row
        hess_ref[at, :] = rows
        widest = widest + jnp.sum(jnp.abs(rows), axis=0, keepdims=True)
    alpha = 1.9 / jnp.max(widest)

    def eye():
        rid = lax.broadcasted_iota(jnp.int32, (M, M), 0)
        cid = lax.broadcasted_iota(jnp.int32, (M, M), 1)
        return (rid == cid).astype(F32)

    first = eye() - alpha * hess_ref[...]
    r_ref[...] = first
    inv_ref[...] = alpha * (eye() + first)

    def double(_, carry):
        r = r_ref[...].astype(BF)
        r2 = jnp.dot(r, r, preferred_element_type=F32)
        r_ref[...] = r2
        inv_ref[...] += jnp.dot(
            inv_ref[...].astype(BF), r2.astype(BF), preferred_element_type=F32
        )
        return carry

    lax.fori_loop(0, DOUBLINGS - 1, double, 0)

    def correct(precise):
        if precise:
            x = inv_ref[...]
            x_high, x_low = split(x)
            product = jnp.dot(
                hess_ref[...], x, precision=lax.Precision.HIGHEST, preferred_element_type=F32
            )
        else:
            x_high = inv_ref[...].astype(BF)
            h_high, h_low = split(hess_ref[...])
            product = jnp.dot(h_high, x_high, preferred_element_type=F32) + jnp.dot(
                h_low, x_high, preferred_element_type=F32
            )
        residual = eye() - product
        size = jnp.sum(residual * residual)
        good = size < M

        @pl.when(good)
        def _():
            r_high, r_low = split(residual)
            if precise:
                inv_ref[...] += times_split(x_high, x_low, r_high, r_low)
            else:
                step = jnp.dot(x_high, r_high, preferred_element_type=F32)
                inv_ref[...] = x_high.astype(F32) + step

        @pl.when(jnp.logical_not(good))
        def _():
            inv_ref[...] = alpha * eye()

        return size

    def correct_again(state):
        return state[0] + 1, correct(True)

    def unfinished(state):
        count, size = state
        return jnp.logical_and(jnp.logical_not(size < ACCEPT), count < MAX_CORRECT)

    correct(False)
    _, size = lax.while_loop(unfinished, correct_again, (jnp.int32(0), jnp.float32(2.0 * M)))

    @pl.when(jnp.logical_not(size < ACCEPT))
    def _():
        inv_ref[...] = hess_ref[...]
        cid = lax.broadcasted_iota(jnp.int32, (8, M), 1)

        def pivot(k, carry):
            row = inv_ref[pl.ds(k, 1), :]
            here = lax.broadcasted_iota(jnp.int32, (1, M), 1) == k
            inverse = 1.0 / jnp.sum(jnp.where(here, row, 0.0))
            row = jnp.where(here, 1.0, row) * inverse

            def sweep(b, inner):
                at = pl.multiple_of(b * 8, 8)
                rows = inv_ref[pl.ds(at, 8), :]
                factor = jnp.sum(jnp.where(cid == k, rows, 0.0), axis=1, keepdims=True)
                rows = jnp.where(cid == k, 0.0, rows) - factor * row
                rid = lax.broadcasted_iota(jnp.int32, (8, M), 0) + at
                inv_ref[pl.ds(at, 8), :] = jnp.where(rid == k, row, rows)
                return inner

            lax.fori_loop(0, M // 8, sweep, 0)
            return carry

        lax.fori_loop(0, M, pivot, 0)

    total = jnp.concatenate(
        [half_ref[0, j, SHARD_G : SHARD_G + 1, :] for j in range(NB)], axis=0
    )
    zero = jnp.zeros((NB, 128), F32)
    lam = newton_update(zero, total, bound_ref[...], inv_ref, scale)
    lam_ref[...] = lam
    product_of_trial(at_ref, pieces, curv_ref, lin_ref, lam_ref, part_ref)


def updated(gathered_ref, lam_in_ref, bound_ref, inv_ref, scale_ref):
    total = jnp.sum(gathered_ref[...], axis=0)
    return newton_update(lam_in_ref[...], total, bound_ref[...], inv_ref, scale_ref[...])


def step_kernel(
    at_ref, own_ref, one_ref, two_ref, three_ref, inv_ref,
    gathered_ref, lam_in_ref, curv_ref, lin_ref, bound_ref, scale_ref,
    lam_ref, part_ref,
):
    lam_ref[...] = updated(gathered_ref, lam_in_ref, bound_ref, inv_ref, scale_ref)
    pieces = (own_ref, one_ref, two_ref, three_ref)
    product_of_trial(at_ref, pieces, curv_ref, lin_ref, lam_ref, part_ref)


def last_kernel(
    at_ref, own_ref, one_ref, two_ref, three_ref, inv_ref,
    gathered_ref, lam_in_ref, curv_ref, lin_ref, bound_ref, scale_ref,
    lam_ref, step_ref,
):
    lam_ref[...] = updated(gathered_ref, lam_in_ref, bound_ref, inv_ref, scale_ref)
    lam_b = as_rows(at_ref, lam_ref)
    pieces = (own_ref, one_ref, two_ref, three_ref)
    count = WIDTH // 128
    for chunk in range(CHUNKS):
        moved = trial_chunk(columns(pieces, chunk), curv_ref, lin_ref, lam_b, chunk)
        for k in range(count):
            at = chunk * count + k
            step_ref[at : at + 1, :] = moved[0:1, k * 128 : (k + 1) * 128]


VM = pl.BlockSpec(memory_space=pltpu.VMEM)
SM = pl.BlockSpec(memory_space=pltpu.SMEM)


def sds(shape, dtype=F32):
    return jax.ShapeDtypeStruct(shape, dtype)


def call(kernel, ins, outs, scratch, mib):
    return pl.pallas_call(
        kernel,
        in_specs=ins,
        out_specs=[VM] * len(outs),
        out_shape=outs,
        scratch_shapes=scratch,
        compiler_params=pltpu.CompilerParams(vmem_limit_bytes=mib * MIB),
    )


def summed(part):
    near = from_everyone(part, NEAR).sum(axis=0)
    return from_everyone(near, FAR)


def on_device(gradients, perm, weights, linear, bound):
    here = lax.axis_index(BRICK)
    quarter = lax.axis_index("grp")
    core = lax.axis_index("brick_2")
    per_brick = gradients.shape[1] // 128
    at = jnp.stack([quarter, core]).astype(jnp.int32)

    near = size_of(NEAR)
    both = lax.all_to_all(
        jnp.concatenate(
            [
                jnp.broadcast_to(vector.reshape(1, BLKS, 128), (near, BLKS, 128))
                for vector in (weights, linear)
            ],
            axis=2,
        ),
        NEAR, 0, 0, tiled=True,
    )

    slices = [
        lax.dynamic_slice(gradients, (0, lax.rem(quarter + k, 4) * COLS), (ROWS, COLS))
        for k in range(NB)
    ]
    *slices, both, perm = lax.optimization_barrier((*slices, both, perm))
    pieces = [slices[0]]
    for k in (1, 2, 3):
        ring = [(i, (i + k) % 4) for i in range(4)]
        pieces.append(lax.ppermute(slices[k], "grp", ring))

    incoming, leaving, back, place = layout_tables(perm, here, per_brick)
    incoming = lax.dynamic_slice_in_dim(incoming, quarter * BLKS, BLKS)
    place = lax.dynamic_slice_in_dim(place, quarter * BLKS, BLKS)
    both = both.reshape(-1, 256)[leaving]
    both = lax.all_to_all(both, FAR, 0, 0, tiled=True)
    both = both[incoming]
    curv, lin, back, place = lax.optimization_barrier((both[:, :128], both[:, 128:], back, place))

    packed = (HALF, SHARD, 128)
    mine, other = call(
        gram_kernel,
        [SM] + [VM] * 6,
        [sds(packed), sds(packed)],
        [
            pltpu.VMEM((M, M), F32),
            pltpu.VMEM((16, M), F32),
            pltpu.VMEM((NB, NB, 128, 128), F32),
            pltpu.VMEM((2, *packed), F32),
        ],
        20,
    )(at, *pieces, curv, lin)

    swap = [(0, 1), (1, 0)]
    mine = mine + lax.ppermute(other, "brick_2", swap)
    shard = lax.all_to_all(mine, PLANE, 0, 0, tiled=True).sum(axis=0)
    shard = from_everyone(shard, "brick_1").sum(axis=0)
    mine = from_everyone(shard, PLANE)
    other = lax.ppermute(mine, "brick_2", swap)

    bound = bound.reshape(NB, 128)
    square = sds((M, M))
    vector = sds((NB, 128))
    inv, scale, lam, part = call(
        solve_kernel,
        [SM] + [VM] * 9,
        [square, vector, vector, vector],
        [
            pltpu.VMEM((2, *packed), F32),
            pltpu.VMEM((M, M), F32),
            pltpu.VMEM((M, M), F32),
        ],
        28,
    )(at, *pieces, mine, other, curv, lin, bound)
    ins = [SM] + [VM] * 11
    for _ in range(ITERS - 2):
        lam, part = call(step_kernel, ins, [vector, vector], [], 16)(
            at, *pieces, inv, summed(part), lam, curv, lin, bound, scale
        )
    lam, result = call(last_kernel, ins, [vector, sds((BLKS, 128))], [], 16)(
        at, *pieces, inv, summed(part), lam, curv, lin, bound, scale
    )

    whole = from_everyone(result, NEAR).reshape(-1, 128)
    arrived = lax.all_to_all(whole[back], FAR, 0, 0, tiled=True)
    return (arrived[place].reshape(-1), lam.reshape(-1))


def solution(mesh):
    torus = Mesh(
        mesh.devices.reshape(4, 8, 2, mesh.shape["grp"]), ("brick_0", "brick_1", "brick_2", "grp")
    )
    placed = (P("grp", BRICK), P(), P(BRICK_GRP), P(BRICK_GRP), P())
    return jax.shard_map(
        on_device, mesh=torus, in_specs=placed, out_specs=(P(BRICK_GRP), P()), check_vma=False
    )
```

```python
import functools

import jax
import jax.numpy as jnp
from jax import lax
from jax.experimental import pallas as pl
from jax.experimental.pallas import tpu as pltpu
from jax.sharding import Mesh
from jax.sharding import PartitionSpec as P


ITERS = 4
BRICK = ("brick_0", "brick_1", "brick_2")
BRICK_GRP = ("brick_0", "brick_1", "brick_2", "grp")
FAR = ("brick_0", "brick_1")
NEAR = ("brick_2", "grp")
PLANE = ("brick_0", "grp")
M = 512
ROWS = 128
NB = M // ROWS
COLS = 4096
BLKS = COLS // 128
NVAR = 1048576
PAIRS = [(i, j) for i in range(NB) for j in range(i + 1)]
SHARDS = 32
SHARD_G = len(PAIRS) * ROWS // SHARDS
SHARD = SHARD_G + 8
HALF = SHARDS // 2
DOUBLINGS = 4
MAX_CORRECT = 48
ACCEPT = 1e-4
TINY = 1e-5

move_limit = 1.0
MIB = 1024 * 1024
BF = jnp.bfloat16
F32 = jnp.float32


def size_of(axis):
    return lax.axis_size(axis)


def from_everyone(array, axis):
    devices = size_of(axis)
    return lax.all_to_all(
        jnp.broadcast_to(array[None], (devices, *array.shape)), axis, 0, 0, tiled=True
    )


def two_of(mask, values):
    index = lax.broadcasted_iota(jnp.int32, values.shape, 1)
    first = jnp.min(jnp.where(mask, index, values.shape[1]), axis=1, keepdims=True)
    second = jnp.max(jnp.where(mask, index, -1), axis=1, keepdims=True)
    kept = [jnp.sum(jnp.where(index == at, values, 0), axis=1) for at in (first, second)]
    return jnp.stack(kept, axis=1)


def ranks(keys):
    return jnp.sum(keys[None, :] < keys[:, None], axis=1, dtype=jnp.int32)


def inverted(places, count):
    slots = jnp.arange(count, dtype=jnp.int32)
    index = jnp.arange(places.shape[0], dtype=jnp.int32)
    return jnp.sum(jnp.where(places[None, :] == slots[:, None], index[None, :], 0), axis=1)


def layout_tables(perm, here, per_brick):
    chip, core = here // 2, here % 2
    per_chip = 2 * per_brick
    grid = perm.reshape(-1, per_brick)
    same = lax.dynamic_index_in_dim(grid.reshape(-1, 2, per_brick), core, 1, keepdims=False)
    rows = jnp.concatenate([grid, same, same], axis=0)
    bricks, chips = grid.shape[0], same.shape[0]
    line = lax.broadcasted_iota(jnp.int32, rows.shape, 0)
    wanted = jnp.where(line < bricks, here, chip * 2 + (line >= bricks + chips))
    picked = two_of(rows // per_brick == wanted, rows)
    incoming = picked[:bricks].reshape(-1) % per_brick
    back = jnp.stack([picked[bricks : bricks + chips], picked[bricks + chips :]], axis=1)
    back = back.reshape(-1) % per_chip
    local = lax.dynamic_slice_in_dim(perm, chip * per_chip, per_chip)
    index = jnp.arange(per_chip, dtype=jnp.int32)
    key = (local // per_chip) * per_chip + index
    key = jnp.where((local // per_brick) % 2 == core, key, key + perm.shape[0] * 2)
    leaving = inverted(ranks(key), per_brick)
    mine = lax.dynamic_slice_in_dim(perm, here * per_brick, per_brick)
    place = ranks((mine // per_brick) * per_brick + jnp.arange(per_brick, dtype=jnp.int32))
    return (inverted(incoming, per_brick), leaving, back, place)


def down(row):
    return jnp.broadcast_to(row, (128, 128)).T


def times(mat_ref, vec):
    total = [jnp.zeros((8, 128), F32) for _ in range(NB)]
    for i in range(NB):
        column = down(vec[i : i + 1, :])
        for j in range(NB):
            part = mat_ref[i * 128 : (i + 1) * 128, j * 128 : (j + 1) * 128] * column
            total[j] = total[j] + part.reshape(16, 8, 128).sum(axis=0)
    return jnp.concatenate([t.sum(axis=0, keepdims=True) for t in total], axis=0)


WIDTH = 1024
CHUNKS = COLS // WIDTH
NT = (((1,), (1,)), ((), ()))


def flat_rows(ref, chunk):
    count = WIDTH // 128
    rows = [ref[chunk * count + k : chunk * count + k + 1, :] for k in range(count)]
    return jnp.concatenate(rows, axis=1)


class Columns:
    def __init__(self, pieces, full_ref, sems):
        self.full_ref = full_ref
        self.copies = []
        for chunk in range(CHUNKS):
            to = pl.ds(chunk * WIDTH, WIDTH)
            self.copies.append(
                [
                    pltpu.make_async_copy(
                        piece.at[:, to], full_ref.at[k, :, to], sems.at[chunk, k]
                    )
                    for k, piece in enumerate(pieces)
                ]
            )
        for group in self.copies:
            for copy in group:
                copy.start()

    def chunk(self, chunk):
        for copy in self.copies[chunk]:
            copy.wait()
        return self.full_ref[:, :, chunk * WIDTH : (chunk + 1) * WIDTH].reshape(M, WIDTH)


def slots(at_ref):
    return [lax.rem(at_ref[0] + NB - k, NB) for k in range(NB)]


def as_rows(at_ref, lam_ref):
    flat = jnp.concatenate([lam_ref[pl.ds(slot, 1), :] for slot in slots(at_ref)], axis=1)
    return jnp.broadcast_to(flat, (16, M)).astype(BF)


def trial_chunk(block, curv_ref, lin_ref, lam_b, chunk):
    pushed = jnp.dot(lam_b, block, preferred_element_type=F32)
    curv, lin = flat_rows(curv_ref, chunk), flat_rows(lin_ref, chunk)
    return jnp.clip(-curv * (lin + pushed), -move_limit, move_limit)


def product_of_trial(at_ref, columns, curv_ref, lin_ref, lam_ref, part_ref):
    lam_b = as_rows(at_ref, lam_ref)
    total = jnp.zeros((16, M), F32)
    for chunk in range(CHUNKS):
        block = columns.chunk(chunk)
        moved = trial_chunk(block, curv_ref, lin_ref, lam_b, chunk).astype(BF)
        total += lax.dot_general(moved, block, NT, preferred_element_type=F32)
    for k, slot in enumerate(slots(at_ref)):
        part_ref[pl.ds(slot, 1), :] = total[0:1, k * 128 : (k + 1) * 128]


def newton_update(lam, total, bound, inv_ref, scale):
    rhs = (total * (1.0 / NVAR) - bound) * scale
    return jnp.maximum(lam + times(inv_ref, rhs) * scale, 0.0)


def packed_tile(p, t):
    tile = p * 16 + t
    shard, row = tile // (SHARD_G // 8), tile % (SHARD_G // 8) * 8
    return shard // HALF, shard % HALF, slice(row, row + 8)


def gram_kernel(
    at_ref, own_hbm, one_hbm, two_hbm, three_hbm, curv_ref, lin_ref,
    mine_ref, other_ref, gram_ref, prod_ref, block_ref, half_ref, full_ref, sems,
):
    core = at_ref[1]
    columns = Columns((own_hbm, one_hbm, two_hbm, three_hbm), full_ref, sems)
    gram_ref[...] = jnp.zeros_like(gram_ref)
    prod_ref[...] = jnp.zeros_like(prod_ref)
    for s in range(SHARDS):
        half_ref[s // HALF, s % HALF, SHARD_G:, :] = jnp.zeros((8, 128), F32)
    for chunk in range(CHUNKS):
        block = columns.chunk(chunk)
        curv, lin = flat_rows(curv_ref, chunk), flat_rows(lin_ref, chunk)
        weighted = (block.astype(F32) * curv).astype(BF)
        gram_ref[...] += lax.dot_general(weighted, block, NT, preferred_element_type=F32)
        moved = jnp.clip(-curv * lin, -move_limit, move_limit)
        moved = jnp.broadcast_to(moved, (16, WIDTH)).astype(BF)
        prod_ref[...] += lax.dot_general(moved, block, NT, preferred_element_type=F32)
    where = slots(at_ref)
    for a in range(NB):
        half_ref[0, pl.ds(where[a], 1), SHARD_G, :] = prod_ref[0:1, a * 128 : (a + 1) * 128]
        for b in range(NB):
            block_ref[where[a], where[b]] = gram_ref[
                a * 128 : (a + 1) * 128, b * 128 : (b + 1) * 128
            ]
    for p, (i, j) in enumerate(PAIRS):
        value = 0.5 * (block_ref[i, j] + block_ref[j, i].T)
        for t in range(16):
            half_ref[packed_tile(p, t)] = value[t * 8 : t * 8 + 8]
    mine_ref[...] = half_ref[core]
    other_ref[...] = half_ref[1 - core]


def split(value):
    high = value.astype(BF)
    return high, (value - high.astype(F32)).astype(BF)


def split_in_three(value):
    high = value.astype(BF)
    middle, low = split(value - high.astype(F32))
    return high, middle, low


def solve_kernel(
    at_ref, own_hbm, one_hbm, two_hbm, three_hbm, mine_ref, other_ref, curv_ref, lin_ref, bound_ref,
    inv_ref, scale_ref, lam_ref, part_ref,
    half_ref, hess_ref, r_ref, full_ref, sems,
):
    columns = Columns((own_hbm, one_hbm, two_hbm, three_hbm), full_ref, sems)
    core = at_ref[1]
    half_ref[core] = mine_ref[...]
    half_ref[1 - core] = other_ref[...]
    for p, (i, j) in enumerate(PAIRS):
        for t in range(16):
            at = i * 128 + t * 8
            hess_ref[at : at + 8, j * 128 : (j + 1) * 128] = half_ref[packed_tile(p, t)] * (
                1.0 / NVAR
            )
    row_id = lax.broadcasted_iota(jnp.int32, (128, 128), 0)
    col_id = lax.broadcasted_iota(jnp.int32, (128, 128), 1)
    diagonal = row_id == col_id
    for i in range(NB):
        at = slice(i * 128, (i + 1) * 128)
        for j in range(i):
            hess_ref[j * 128 : (j + 1) * 128, at] = hess_ref[at, j * 128 : (j + 1) * 128].T
        values = jnp.sum(jnp.where(diagonal, hess_ref[at, at], 0.0), axis=0, keepdims=True)
        scale_ref[i : i + 1, :] = lax.rsqrt(values)
    scale = scale_ref[...]
    scale_row = jnp.concatenate([scale[i : i + 1, :] for i in range(NB)], axis=1)
    widest = jnp.zeros((1, M), F32)
    for i in range(NB):
        at = slice(i * 128, (i + 1) * 128)
        column = jnp.concatenate([down(scale[i : i + 1, :])] * NB, axis=1)
        rows = hess_ref[at, :] * column * scale_row
        hess_ref[at, :] = rows
        widest = widest + jnp.sum(jnp.abs(rows), axis=0, keepdims=True)
    alpha = 1.9 / jnp.max(widest)

    def eye():
        rid = lax.broadcasted_iota(jnp.int32, (M, M), 0)
        cid = lax.broadcasted_iota(jnp.int32, (M, M), 1)
        return (rid == cid).astype(F32)

    first = eye() - alpha * hess_ref[...]
    r_ref[...] = first
    inv_ref[...] = alpha * (eye() + first)

    def double(_, carry):
        r = r_ref[...].astype(BF)
        r2 = jnp.dot(r, r, preferred_element_type=F32)
        r_ref[...] = r2
        inv_ref[...] += jnp.dot(
            inv_ref[...].astype(BF), r2.astype(BF), preferred_element_type=F32
        )
        return carry

    lax.fori_loop(0, DOUBLINGS - 1, double, 0)

    def correct(precise):
        dot = functools.partial(jnp.dot, preferred_element_type=F32)
        x_high, x_low = split(inv_ref[...])
        h_high, h_low, h_rest = split_in_three(hess_ref[...])
        product = dot(h_high, x_high)
        if precise:
            product += dot(h_high, x_low) + (
                dot(h_low, x_high) + (dot(h_low, x_low) + dot(h_rest, x_high))
            )
        else:
            product += dot(h_low, x_high)
        residual = eye() - product
        size = jnp.sum(residual * residual)
        good = size < M

        @pl.when(good)
        def _():
            r_high, r_low = split(residual)
            step = dot(x_high, r_high)
            inv_ref[...] = x_high.astype(F32) + step
            if precise:
                inv_ref[...] += x_low.astype(F32)

            if precise:

                @pl.when(size > TINY)
                def _():
                    inv_ref[...] += dot(x_high, r_low) + dot(x_low, r_high)

        @pl.when(jnp.logical_not(good))
        def _():
            inv_ref[...] = alpha * eye()

        return size

    def correct_again(state):
        return state[0] + 1, correct(True)

    def unfinished(state):
        count, size = state
        return jnp.logical_and(jnp.logical_not(size < ACCEPT), count < MAX_CORRECT)

    correct(False)
    _, size = lax.while_loop(unfinished, correct_again, (jnp.int32(0), jnp.float32(2.0 * M)))

    @pl.when(jnp.logical_not(size < ACCEPT))
    def _():
        inv_ref[...] = hess_ref[...]
        cid = lax.broadcasted_iota(jnp.int32, (8, M), 1)

        def pivot(k, carry):
            row = inv_ref[pl.ds(k, 1), :]
            here = lax.broadcasted_iota(jnp.int32, (1, M), 1) == k
            inverse = 1.0 / jnp.sum(jnp.where(here, row, 0.0))
            row = jnp.where(here, 1.0, row) * inverse

            def sweep(b, inner):
                at = pl.multiple_of(b * 8, 8)
                rows = inv_ref[pl.ds(at, 8), :]
                factor = jnp.sum(jnp.where(cid == k, rows, 0.0), axis=1, keepdims=True)
                rows = jnp.where(cid == k, 0.0, rows) - factor * row
                rid = lax.broadcasted_iota(jnp.int32, (8, M), 0) + at
                inv_ref[pl.ds(at, 8), :] = jnp.where(rid == k, row, rows)
                return inner

            lax.fori_loop(0, M // 8, sweep, 0)
            return carry

        lax.fori_loop(0, M, pivot, 0)

    total = jnp.concatenate(
        [half_ref[0, j, SHARD_G : SHARD_G + 1, :] for j in range(NB)], axis=0
    )
    zero = jnp.zeros((NB, 128), F32)
    lam = newton_update(zero, total, bound_ref[...], inv_ref, scale)
    lam_ref[...] = lam
    product_of_trial(at_ref, columns, curv_ref, lin_ref, lam_ref, part_ref)


def updated(gathered_ref, lam_in_ref, bound_ref, inv_ref, scale_ref):
    total = jnp.sum(gathered_ref[...], axis=0)
    return newton_update(lam_in_ref[...], total, bound_ref[...], inv_ref, scale_ref[...])


def step_kernel(
    at_ref, own_hbm, one_hbm, two_hbm, three_hbm, inv_ref,
    gathered_ref, lam_in_ref, curv_ref, lin_ref, bound_ref, scale_ref,
    lam_ref, part_ref, full_ref, sems,
):
    columns = Columns((own_hbm, one_hbm, two_hbm, three_hbm), full_ref, sems)
    lam_ref[...] = updated(gathered_ref, lam_in_ref, bound_ref, inv_ref, scale_ref)
    product_of_trial(at_ref, columns, curv_ref, lin_ref, lam_ref, part_ref)


def last_kernel(
    at_ref, own_hbm, one_hbm, two_hbm, three_hbm, inv_ref,
    gathered_ref, lam_in_ref, curv_ref, lin_ref, bound_ref, scale_ref,
    lam_ref, step_ref, full_ref, sems,
):
    columns = Columns((own_hbm, one_hbm, two_hbm, three_hbm), full_ref, sems)
    lam_ref[...] = updated(gathered_ref, lam_in_ref, bound_ref, inv_ref, scale_ref)
    lam_b = as_rows(at_ref, lam_ref)
    count = WIDTH // 128
    for chunk in range(CHUNKS):
        moved = trial_chunk(columns.chunk(chunk), curv_ref, lin_ref, lam_b, chunk)
        for k in range(count):
            at = chunk * count + k
            for copy in range(step_ref.shape[0]):
                step_ref[copy, at : at + 1, :] = moved[0:1, k * 128 : (k + 1) * 128]


VM = pl.BlockSpec(memory_space=pltpu.VMEM)
HBM = pl.BlockSpec(memory_space=pltpu.HBM)
FULL = [pltpu.VMEM((NB, ROWS, COLS), BF), pltpu.SemaphoreType.DMA((CHUNKS, NB))]
SM = pl.BlockSpec(memory_space=pltpu.SMEM)


def sds(shape, dtype=F32):
    return jax.ShapeDtypeStruct(shape, dtype)


def call(kernel, ins, outs, scratch, mib):
    return pl.pallas_call(
        kernel,
        in_specs=ins,
        out_specs=[VM] * len(outs),
        out_shape=outs,
        scratch_shapes=scratch,
        compiler_params=pltpu.CompilerParams(vmem_limit_bytes=mib * MIB),
    )


def summed(part):
    near = from_everyone(part, NEAR).sum(axis=0)
    return from_everyone(near, FAR)


def on_device(gradients, perm, weights, linear, bound):
    here = lax.axis_index(BRICK)
    quarter = lax.axis_index("grp")
    core = lax.axis_index("brick_2")
    per_brick = gradients.shape[1] // 128
    at = jnp.stack([quarter, core]).astype(jnp.int32)

    near = size_of(NEAR)
    both = jnp.concatenate([weights.reshape(1, BLKS, 128), linear.reshape(1, BLKS, 128)], axis=2)
    both = jnp.broadcast_to(both, (near, BLKS, 256))
    both = lax.all_to_all(both, NEAR, 0, 0, tiled=True)

    pieces, last = [None] * NB, gradients
    for k in (1, 3, 2, 0):
        to = lax.rem(quarter + k, NB) * COLS
        piece = lax.dynamic_slice(last, (0, to), (ROWS, COLS))
        piece, last = lax.optimization_barrier((piece, last))
        if k:
            piece = lax.ppermute(piece, "grp", [(i, (i + k) % NB) for i in range(NB)])
        pieces[k] = piece
    both, perm = lax.optimization_barrier((both, perm))

    incoming, leaving, back, place = layout_tables(perm, here, per_brick)
    incoming = lax.dynamic_slice_in_dim(incoming, quarter * BLKS, BLKS)
    place = lax.dynamic_slice_in_dim(place, quarter * BLKS, BLKS)
    both = both.reshape(-1, 256)[leaving]
    both = lax.all_to_all(both, FAR, 0, 0, tiled=True)
    both = both[incoming]
    curv, lin, back, place = lax.optimization_barrier((both[:, :128], both[:, 128:], back, place))

    packed = (HALF, SHARD, 128)
    mine, other = call(
        gram_kernel,
        [SM] + [HBM] * NB + [VM] * 2,
        [sds(packed), sds(packed)],
        [
            pltpu.VMEM((M, M), F32),
            pltpu.VMEM((16, M), F32),
            pltpu.VMEM((NB, NB, 128, 128), F32),
            pltpu.VMEM((2, *packed), F32),
            *FULL,
        ],
        24,
    )(at, *pieces, curv, lin)

    pieces = [pltpu.with_memory_space_constraint(piece, pltpu.HBM) for piece in pieces]

    swap = [(0, 1), (1, 0)]
    mine = mine + lax.ppermute(other, "brick_2", swap)
    shard = lax.all_to_all(mine, PLANE, 0, 0, tiled=True).sum(axis=0)
    shard = from_everyone(shard, "brick_1").sum(axis=0)
    mine = from_everyone(shard, PLANE)
    other = lax.ppermute(mine, "brick_2", swap)

    bound = bound.reshape(NB, 128)
    square = sds((M, M))
    vector = sds((NB, 128))
    inv, scale, lam, part = call(
        solve_kernel,
        [SM] + [HBM] * NB + [VM] * 5,
        [square, vector, vector, vector],
        [
            pltpu.VMEM((2, *packed), F32),
            pltpu.VMEM((M, M), F32),
            pltpu.VMEM((M, M), F32),
            *FULL,
        ],
        32,
    )(at, *pieces, mine, other, curv, lin, bound)
    ins = [SM] + [HBM] * NB + [VM] * 7
    for _ in range(ITERS - 2):
        lam, part = call(step_kernel, ins, [vector, vector], FULL, 20)(
            at, *pieces, inv, summed(part), lam, curv, lin, bound, scale
        )
    lam, result = call(last_kernel, ins, [vector, sds((size_of(NEAR), BLKS, 128))], FULL, 20)(
        at, *pieces, inv, summed(part), lam, curv, lin, bound, scale
    )

    whole = lax.all_to_all(result, NEAR, 0, 0, tiled=True).reshape(-1, 128)
    arrived = lax.all_to_all(whole[back], FAR, 0, 0, tiled=True)
    return (arrived[place].reshape(-1), lam.reshape(-1))


def solution(mesh):
    torus = Mesh(
        mesh.devices.reshape(4, 8, 2, mesh.shape["grp"]), ("brick_0", "brick_1", "brick_2", "grp")
    )
    placed = (P("grp", BRICK), P(), P(BRICK_GRP), P(BRICK_GRP), P())
    return jax.shard_map(
        on_device, mesh=torus, in_specs=placed, out_specs=(P(BRICK_GRP), P()), check_vma=False
    )
```

```python
import functools

import jax
import jax.numpy as jnp
from jax import lax
from jax.experimental import pallas as pl
from jax.experimental.pallas import tpu as pltpu
from jax.sharding import Mesh
from jax.sharding import PartitionSpec as P


ITERS = 4
BRICK = ("brick_0", "brick_1", "brick_2")
BRICK_GRP = ("brick_0", "brick_1", "brick_2", "grp")
FAR = ("brick_0", "brick_1")
NEAR = ("brick_2", "grp")
PLANE = ("brick_0", "grp")
M = 512
ROWS = 128
NB = M // ROWS
COLS = 4096
BLKS = COLS // 128
NVAR = 1048576
PAIRS = [(i, j) for i in range(NB) for j in range(i + 1)]
SHARDS = 32
SHARD_G = len(PAIRS) * ROWS // SHARDS
SHARD = SHARD_G + 8
HALF = SHARDS // 2
DOUBLINGS = 4
MAX_CORRECT = 48
ACCEPT = 1e-4
TINY = 1e-5

move_limit = 1.0
MIB = 1024 * 1024
BF = jnp.bfloat16
F32 = jnp.float32


def size_of(axis):
    return lax.axis_size(axis)


def from_everyone(array, axis):
    devices = size_of(axis)
    return lax.all_to_all(
        jnp.broadcast_to(array[None], (devices, *array.shape)), axis, 0, 0, tiled=True
    )


def two_of(mask, values):
    index = lax.broadcasted_iota(jnp.int32, values.shape, 1)
    first = jnp.min(jnp.where(mask, index, values.shape[1]), axis=1, keepdims=True)
    second = jnp.max(jnp.where(mask, index, -1), axis=1, keepdims=True)
    kept = [jnp.sum(jnp.where(index == at, values, 0), axis=1) for at in (first, second)]
    return jnp.stack(kept, axis=1)


def ranks(keys):
    return jnp.sum(keys[None, :] < keys[:, None], axis=1, dtype=jnp.int32)


def inverted(places, count):
    slots = jnp.arange(count, dtype=jnp.int32)
    index = jnp.arange(places.shape[0], dtype=jnp.int32)
    return jnp.sum(jnp.where(places[None, :] == slots[:, None], index[None, :], 0), axis=1)


def layout_tables(perm, here, per_brick):
    chip, core = here // 2, here % 2
    per_chip = 2 * per_brick
    grid = perm.reshape(-1, per_brick)
    same = lax.dynamic_index_in_dim(grid.reshape(-1, 2, per_brick), core, 1, keepdims=False)
    rows = jnp.concatenate([grid, same, same], axis=0)
    bricks, chips = grid.shape[0], same.shape[0]
    line = lax.broadcasted_iota(jnp.int32, rows.shape, 0)
    wanted = jnp.where(line < bricks, here, chip * 2 + (line >= bricks + chips))
    picked = two_of(rows // per_brick == wanted, rows)
    incoming = picked[:bricks].reshape(-1) % per_brick
    back = jnp.stack([picked[bricks : bricks + chips], picked[bricks + chips :]], axis=1)
    back = back.reshape(-1) % per_chip
    local = lax.dynamic_slice_in_dim(perm, chip * per_chip, per_chip)
    index = jnp.arange(per_chip, dtype=jnp.int32)
    key = (local // per_chip) * per_chip + index
    key = jnp.where((local // per_brick) % 2 == core, key, key + perm.shape[0] * 2)
    leaving = inverted(ranks(key), per_brick)
    mine = lax.dynamic_slice_in_dim(perm, here * per_brick, per_brick)
    place = ranks((mine // per_brick) * per_brick + jnp.arange(per_brick, dtype=jnp.int32))
    return (inverted(incoming, per_brick), leaving, back, place)


def down(row):
    return jnp.broadcast_to(row, (128, 128)).T


def times(mat_ref, vec):
    total = [jnp.zeros((8, 128), F32) for _ in range(NB)]
    for i in range(NB):
        column = down(vec[i : i + 1, :])
        for j in range(NB):
            part = mat_ref[i * 128 : (i + 1) * 128, j * 128 : (j + 1) * 128] * column
            total[j] = total[j] + part.reshape(16, 8, 128).sum(axis=0)
    return jnp.concatenate([t.sum(axis=0, keepdims=True) for t in total], axis=0)


WIDTH = 1024
CHUNKS = COLS // WIDTH
NT = (((1,), (1,)), ((), ()))


def flat_rows(ref, chunk):
    count = WIDTH // 128
    rows = [ref[chunk * count + k : chunk * count + k + 1, :] for k in range(count)]
    return jnp.concatenate(rows, axis=1)


class Columns:
    def __init__(self, pieces, full_ref, sems):
        self.full_ref = full_ref
        self.copies = []
        for chunk in range(CHUNKS):
            to = pl.ds(chunk * WIDTH, WIDTH)
            self.copies.append(
                [
                    pltpu.make_async_copy(
                        piece.at[:, to], full_ref.at[k, :, to], sems.at[chunk, k]
                    )
                    for k, piece in enumerate(pieces)
                ]
            )
        for group in self.copies:
            for copy in group:
                copy.start()

    def chunk(self, chunk):
        for copy in self.copies[chunk]:
            copy.wait()
        return self.full_ref[:, :, chunk * WIDTH : (chunk + 1) * WIDTH].reshape(M, WIDTH)


def slots(at_ref):
    return [lax.rem(at_ref[0] + NB - k, NB) for k in range(NB)]


def as_rows(at_ref, lam_ref):
    flat = jnp.concatenate([lam_ref[pl.ds(slot, 1), :] for slot in slots(at_ref)], axis=1)
    return jnp.broadcast_to(flat, (16, M)).astype(BF)


def trial_chunk(block, curv_ref, lin_ref, lam_b, chunk):
    pushed = jnp.dot(lam_b, block, preferred_element_type=F32)
    curv, lin = flat_rows(curv_ref, chunk), flat_rows(lin_ref, chunk)
    return jnp.clip(-curv * (lin + pushed), -move_limit, move_limit)


def product_of_trial(at_ref, columns, curv_ref, lin_ref, lam_ref, part_ref):
    lam_b = as_rows(at_ref, lam_ref)
    total = jnp.zeros((16, M), F32)
    for chunk in range(CHUNKS):
        block = columns.chunk(chunk)
        moved = trial_chunk(block, curv_ref, lin_ref, lam_b, chunk).astype(BF)
        total += lax.dot_general(moved, block, NT, preferred_element_type=F32)
    for k, slot in enumerate(slots(at_ref)):
        part_ref[pl.ds(slot, 1), :] = total[0:1, k * 128 : (k + 1) * 128]


def newton_update(lam, total, bound, inv_ref, scale):
    rhs = (total * (1.0 / NVAR) - bound) * scale
    return jnp.maximum(lam + times(inv_ref, rhs) * scale, 0.0)


def packed_tile(p, t):
    tile = p * 16 + t
    shard, row = tile // (SHARD_G // 8), tile % (SHARD_G // 8) * 8
    return shard // HALF, shard % HALF, slice(row, row + 8)


def gram_kernel(
    at_ref, own_hbm, one_hbm, two_hbm, three_hbm, curv_ref, lin_ref,
    mine_ref, other_ref, gram_ref, prod_ref, block_ref, half_ref, full_ref, sems,
):
    core = at_ref[1]
    columns = Columns((own_hbm, one_hbm, two_hbm, three_hbm), full_ref, sems)
    gram_ref[...] = jnp.zeros_like(gram_ref)
    prod_ref[...] = jnp.zeros_like(prod_ref)
    for s in range(SHARDS):
        half_ref[s // HALF, s % HALF, SHARD_G:, :] = jnp.zeros((8, 128), F32)
    for chunk in range(CHUNKS):
        block = columns.chunk(chunk)
        curv, lin = flat_rows(curv_ref, chunk), flat_rows(lin_ref, chunk)
        weighted = (block.astype(F32) * curv).astype(BF)
        gram_ref[...] += lax.dot_general(weighted, block, NT, preferred_element_type=F32)
        moved = jnp.clip(-curv * lin, -move_limit, move_limit)
        moved = jnp.broadcast_to(moved, (16, WIDTH)).astype(BF)
        prod_ref[...] += lax.dot_general(moved, block, NT, preferred_element_type=F32)
    where = slots(at_ref)
    for a in range(NB):
        half_ref[0, pl.ds(where[a], 1), SHARD_G, :] = prod_ref[0:1, a * 128 : (a + 1) * 128]
        for b in range(NB):
            block_ref[where[a], where[b]] = gram_ref[
                a * 128 : (a + 1) * 128, b * 128 : (b + 1) * 128
            ]
    for p, (i, j) in enumerate(PAIRS):
        value = 0.5 * (block_ref[i, j] + block_ref[j, i].T)
        for t in range(16):
            half_ref[packed_tile(p, t)] = value[t * 8 : t * 8 + 8]
    mine_ref[...] = half_ref[core]
    other_ref[...] = half_ref[1 - core]


def split(value):
    high = value.astype(BF)
    return high, (value - high.astype(F32)).astype(BF)


def split_in_three(value):
    high = value.astype(BF)
    middle, low = split(value - high.astype(F32))
    return high, middle, low


def solve_kernel(
    at_ref, own_hbm, one_hbm, two_hbm, three_hbm, mine_ref, other_ref, curv_ref, lin_ref, bound_ref,
    inv_ref, scale_ref, lam_ref, part_ref,
    half_ref, hess_ref, r_ref, full_ref, sems,
):
    columns = Columns((own_hbm, one_hbm, two_hbm, three_hbm), full_ref, sems)
    core = at_ref[1]
    half_ref[core] = mine_ref[...]
    half_ref[1 - core] = other_ref[...]
    for p, (i, j) in enumerate(PAIRS):
        for t in range(16):
            at = i * 128 + t * 8
            hess_ref[at : at + 8, j * 128 : (j + 1) * 128] = half_ref[packed_tile(p, t)] * (
                1.0 / NVAR
            )
    row_id = lax.broadcasted_iota(jnp.int32, (128, 128), 0)
    col_id = lax.broadcasted_iota(jnp.int32, (128, 128), 1)
    diagonal = row_id == col_id
    for i in range(NB):
        at = slice(i * 128, (i + 1) * 128)
        for j in range(i):
            hess_ref[j * 128 : (j + 1) * 128, at] = hess_ref[at, j * 128 : (j + 1) * 128].T
        values = jnp.sum(jnp.where(diagonal, hess_ref[at, at], 0.0), axis=0, keepdims=True)
        scale_ref[i : i + 1, :] = lax.rsqrt(values)
    scale = scale_ref[...]
    scale_row = jnp.concatenate([scale[i : i + 1, :] for i in range(NB)], axis=1)
    widest = jnp.zeros((1, M), F32)
    for i in range(NB):
        at = slice(i * 128, (i + 1) * 128)
        column = jnp.concatenate([down(scale[i : i + 1, :])] * NB, axis=1)
        rows = hess_ref[at, :] * column * scale_row
        hess_ref[at, :] = rows
        widest = widest + jnp.sum(jnp.abs(rows), axis=0, keepdims=True)
    alpha = 1.9 / jnp.max(widest)

    def eye():
        rid = lax.broadcasted_iota(jnp.int32, (M, M), 0)
        cid = lax.broadcasted_iota(jnp.int32, (M, M), 1)
        return (rid == cid).astype(F32)

    first = eye() - alpha * hess_ref[...]
    r_ref[...] = first
    inv_ref[...] = alpha * (eye() + first)

    def double(_, carry):
        r = r_ref[...].astype(BF)
        r2 = jnp.dot(r, r, preferred_element_type=F32)
        r_ref[...] = r2
        inv_ref[...] += jnp.dot(
            inv_ref[...].astype(BF), r2.astype(BF), preferred_element_type=F32
        )
        return carry

    lax.fori_loop(0, DOUBLINGS - 1, double, 0)

    def correct(precise):
        dot = functools.partial(jnp.dot, preferred_element_type=F32)
        x_high, x_low = split(inv_ref[...])
        h_high, h_low, h_rest = split_in_three(hess_ref[...])
        product = dot(h_high, x_high)
        if precise:
            product += dot(h_high, x_low) + (
                dot(h_low, x_high) + (dot(h_low, x_low) + dot(h_rest, x_high))
            )
        else:
            product += dot(h_low, x_high)
        residual = eye() - product
        size = jnp.sum(residual * residual)
        good = size < M

        @pl.when(good)
        def _():
            r_high, r_low = split(residual)
            step = dot(x_high, r_high)
            inv_ref[...] = x_high.astype(F32) + step
            if precise:
                inv_ref[...] += x_low.astype(F32)

            if precise:

                @pl.when(size > TINY)
                def _():
                    inv_ref[...] += dot(x_high, r_low) + dot(x_low, r_high)

        @pl.when(jnp.logical_not(good))
        def _():
            inv_ref[...] = alpha * eye()

        return size

    def correct_again(state):
        return state[0] + 1, correct(True)

    def unfinished(state):
        count, size = state
        return jnp.logical_and(jnp.logical_not(size < ACCEPT), count < MAX_CORRECT)

    correct(False)
    _, size = lax.while_loop(unfinished, correct_again, (jnp.int32(0), jnp.float32(2.0 * M)))

    @pl.when(jnp.logical_not(size < ACCEPT))
    def _():
        inv_ref[...] = hess_ref[...]
        cid = lax.broadcasted_iota(jnp.int32, (8, M), 1)

        def pivot(k, carry):
            row = inv_ref[pl.ds(k, 1), :]
            here = lax.broadcasted_iota(jnp.int32, (1, M), 1) == k
            inverse = 1.0 / jnp.sum(jnp.where(here, row, 0.0))
            row = jnp.where(here, 1.0, row) * inverse

            def sweep(b, inner):
                at = pl.multiple_of(b * 8, 8)
                rows = inv_ref[pl.ds(at, 8), :]
                factor = jnp.sum(jnp.where(cid == k, rows, 0.0), axis=1, keepdims=True)
                rows = jnp.where(cid == k, 0.0, rows) - factor * row
                rid = lax.broadcasted_iota(jnp.int32, (8, M), 0) + at
                inv_ref[pl.ds(at, 8), :] = jnp.where(rid == k, row, rows)
                return inner

            lax.fori_loop(0, M // 8, sweep, 0)
            return carry

        lax.fori_loop(0, M, pivot, 0)

    total = jnp.concatenate(
        [half_ref[0, j, SHARD_G : SHARD_G + 1, :] for j in range(NB)], axis=0
    )
    zero = jnp.zeros((NB, 128), F32)
    lam = newton_update(zero, total, bound_ref[...], inv_ref, scale)
    lam_ref[...] = lam
    product_of_trial(at_ref, columns, curv_ref, lin_ref, lam_ref, part_ref)


def updated(gathered_ref, lam_in_ref, bound_ref, inv_ref, scale_ref):
    total = jnp.sum(gathered_ref[...], axis=0)
    return newton_update(lam_in_ref[...], total, bound_ref[...], inv_ref, scale_ref[...])


def step_kernel(
    at_ref, own_hbm, one_hbm, two_hbm, three_hbm, inv_ref,
    gathered_ref, lam_in_ref, curv_ref, lin_ref, bound_ref, scale_ref,
    lam_ref, part_ref, full_ref, sems,
):
    columns = Columns((own_hbm, one_hbm, two_hbm, three_hbm), full_ref, sems)
    lam_ref[...] = updated(gathered_ref, lam_in_ref, bound_ref, inv_ref, scale_ref)
    product_of_trial(at_ref, columns, curv_ref, lin_ref, lam_ref, part_ref)


def last_kernel(
    at_ref, own_hbm, one_hbm, two_hbm, three_hbm, inv_ref,
    gathered_ref, lam_in_ref, curv_ref, lin_ref, bound_ref, scale_ref,
    lam_ref, step_ref, full_ref, sems,
):
    columns = Columns((own_hbm, one_hbm, two_hbm, three_hbm), full_ref, sems)
    lam_ref[...] = updated(gathered_ref, lam_in_ref, bound_ref, inv_ref, scale_ref)
    lam_b = as_rows(at_ref, lam_ref)
    count = WIDTH // 128
    for chunk in range(CHUNKS):
        moved = trial_chunk(columns.chunk(chunk), curv_ref, lin_ref, lam_b, chunk)
        lines = [moved[0:1, k * 128 : (k + 1) * 128] for k in range(count)]
        lines = jnp.concatenate(lines, axis=0)
        for copy in range(step_ref.shape[0]):
            step_ref[copy, chunk * count : (chunk + 1) * count, :] = lines


VM = pl.BlockSpec(memory_space=pltpu.VMEM)
HBM = pl.BlockSpec(memory_space=pltpu.HBM)
FULL = [pltpu.VMEM((NB, ROWS, COLS), BF), pltpu.SemaphoreType.DMA((CHUNKS, NB))]
SM = pl.BlockSpec(memory_space=pltpu.SMEM)


def sds(shape, dtype=F32):
    return jax.ShapeDtypeStruct(shape, dtype)


def call(kernel, ins, outs, scratch, mib):
    return pl.pallas_call(
        kernel,
        in_specs=ins,
        out_specs=[VM] * len(outs),
        out_shape=outs,
        scratch_shapes=scratch,
        compiler_params=pltpu.CompilerParams(vmem_limit_bytes=mib * MIB),
    )


def summed(part):
    near = from_everyone(part, NEAR).sum(axis=0)
    return from_everyone(near, FAR)


def on_device(gradients, perm, weights, linear, bound):
    here = lax.axis_index(BRICK)
    quarter = lax.axis_index("grp")
    core = lax.axis_index("brick_2")
    per_brick = gradients.shape[1] // 128
    at = jnp.stack([quarter, core]).astype(jnp.int32)

    near = size_of(NEAR)
    pieces, last = [None] * NB, gradients
    for k in (1, 3, 2, 0):
        to = lax.rem(quarter + k, NB) * COLS
        piece = lax.dynamic_slice(last, (0, to), (ROWS, COLS))
        piece, last = lax.optimization_barrier((piece, last))
        if k:
            piece = lax.ppermute(piece, "grp", [(i, (i + k) % NB) for i in range(NB)])
        pieces[k] = piece
    both = jnp.concatenate([weights.reshape(1, BLKS, 128), linear.reshape(1, BLKS, 128)], axis=2)
    both = jnp.broadcast_to(both, (near, BLKS, 256))
    both = lax.all_to_all(both, NEAR, 0, 0, tiled=True)

    incoming, leaving, back, place = layout_tables(perm, here, per_brick)
    incoming = lax.dynamic_slice_in_dim(incoming, quarter * BLKS, BLKS)
    place = lax.dynamic_slice_in_dim(place, quarter * BLKS, BLKS)
    both = both.reshape(-1, 256)[leaving]
    both = lax.all_to_all(both, FAR, 0, 0, tiled=True)
    both = both[incoming]
    curv, lin, back, place = lax.optimization_barrier((both[:, :128], both[:, 128:], back, place))

    packed = (HALF, SHARD, 128)
    mine, other = call(
        gram_kernel,
        [SM] + [HBM] * NB + [VM] * 2,
        [sds(packed), sds(packed)],
        [
            pltpu.VMEM((M, M), F32),
            pltpu.VMEM((16, M), F32),
            pltpu.VMEM((NB, NB, 128, 128), F32),
            pltpu.VMEM((2, *packed), F32),
            *FULL,
        ],
        24,
    )(at, *pieces, curv, lin)

    pieces = pieces[:2] + [
        pltpu.with_memory_space_constraint(piece, pltpu.HBM) for piece in pieces[2:]
    ]

    swap = [(0, 1), (1, 0)]
    mine = mine + lax.ppermute(other, "brick_2", swap)
    shard = lax.all_to_all(mine, PLANE, 0, 0, tiled=True).sum(axis=0)
    shard = from_everyone(shard, "brick_1").sum(axis=0)
    mine = from_everyone(shard, PLANE)
    other = lax.ppermute(mine, "brick_2", swap)

    bound = bound.reshape(NB, 128)
    square = sds((M, M))
    vector = sds((NB, 128))
    inv, scale, lam, part = call(
        solve_kernel,
        [SM] + [HBM] * NB + [VM] * 5,
        [square, vector, vector, vector],
        [
            pltpu.VMEM((2, *packed), F32),
            pltpu.VMEM((M, M), F32),
            pltpu.VMEM((M, M), F32),
            *FULL,
        ],
        32,
    )(at, *pieces, mine, other, curv, lin, bound)
    ins = [SM] + [HBM] * NB + [VM] * 7
    for _ in range(ITERS - 2):
        lam, part = call(step_kernel, ins, [vector, vector], FULL, 20)(
            at, *pieces, inv, summed(part), lam, curv, lin, bound, scale
        )
    lam, result = call(last_kernel, ins, [vector, sds((size_of(NEAR), BLKS, 128))], FULL, 20)(
        at, *pieces, inv, summed(part), lam, curv, lin, bound, scale
    )

    whole = lax.all_to_all(result, NEAR, 0, 0, tiled=True).reshape(-1, 128)
    arrived = lax.all_to_all(whole[back], FAR, 0, 0, tiled=True)
    return (arrived[place].reshape(-1), lam.reshape(-1))


def solution(mesh):
    torus = Mesh(
        mesh.devices.reshape(4, 8, 2, mesh.shape["grp"]), ("brick_0", "brick_1", "brick_2", "grp")
    )
    placed = (P("grp", BRICK), P(), P(BRICK_GRP), P(BRICK_GRP), P())
    return jax.shard_map(
        on_device, mesh=torus, in_specs=placed, out_specs=(P(BRICK_GRP), P()), check_vma=False
    )
```

```python
import functools

import jax
import jax.numpy as jnp
from jax import lax
from jax.experimental import pallas as pl
from jax.experimental.pallas import tpu as pltpu
from jax.sharding import Mesh
from jax.sharding import PartitionSpec as P


ITERS = 4
BRICK = ("brick_0", "brick_1", "brick_2")
BRICK_GRP = ("brick_0", "brick_1", "brick_2", "grp")
FAR = ("brick_0", "brick_1")
NEAR = ("brick_2", "grp")
PLANE = ("brick_0", "grp")
M = 512
ROWS = 128
NB = M // ROWS
COLS = 4096
BLKS = COLS // 128
NVAR = 1048576
PAIRS = [(i, j) for i in range(NB) for j in range(i + 1)]
SHARDS = 32
SHARD_G = len(PAIRS) * ROWS // SHARDS
SHARD = SHARD_G + 8
HALF = SHARDS // 2
DOUBLINGS = 4
MAX_CORRECT = 48
ACCEPT = 1e-4
TINY = 1e-5

move_limit = 1.0
MIB = 1024 * 1024
BF = jnp.bfloat16
F32 = jnp.float32


def size_of(axis):
    return lax.axis_size(axis)


def from_everyone(array, axis):
    devices = size_of(axis)
    return lax.all_to_all(
        jnp.broadcast_to(array[None], (devices, *array.shape)), axis, 0, 0, tiled=True
    )


def two_of(mask, values):
    index = lax.broadcasted_iota(jnp.int32, values.shape, 1)
    first = jnp.min(jnp.where(mask, index, values.shape[1]), axis=1, keepdims=True)
    second = jnp.max(jnp.where(mask, index, -1), axis=1, keepdims=True)
    kept = [jnp.sum(jnp.where(index == at, values, 0), axis=1) for at in (first, second)]
    return jnp.stack(kept, axis=1)


def ranks(keys):
    return jnp.sum(keys[None, :] < keys[:, None], axis=1, dtype=jnp.int32)


def inverted(places, count):
    slots = jnp.arange(count, dtype=jnp.int32)
    index = jnp.arange(places.shape[0], dtype=jnp.int32)
    return jnp.sum(jnp.where(places[None, :] == slots[:, None], index[None, :], 0), axis=1)


def layout_tables(perm, here, per_brick):
    chip, core = here // 2, here % 2
    per_chip = 2 * per_brick
    grid = perm.reshape(-1, per_brick)
    same = lax.dynamic_index_in_dim(grid.reshape(-1, 2, per_brick), core, 1, keepdims=False)
    rows = jnp.concatenate([grid, same, same], axis=0)
    bricks, chips = grid.shape[0], same.shape[0]
    line = lax.broadcasted_iota(jnp.int32, rows.shape, 0)
    wanted = jnp.where(line < bricks, here, chip * 2 + (line >= bricks + chips))
    picked = two_of(rows // per_brick == wanted, rows)
    incoming = picked[:bricks].reshape(-1) % per_brick
    back = jnp.stack([picked[bricks : bricks + chips], picked[bricks + chips :]], axis=1)
    back = back.reshape(-1) % per_chip
    local = lax.dynamic_slice_in_dim(perm, chip * per_chip, per_chip)
    index = jnp.arange(per_chip, dtype=jnp.int32)
    key = (local // per_chip) * per_chip + index
    key = jnp.where((local // per_brick) % 2 == core, key, key + perm.shape[0] * 2)
    leaving = inverted(ranks(key), per_brick)
    mine = lax.dynamic_slice_in_dim(perm, here * per_brick, per_brick)
    place = ranks((mine // per_brick) * per_brick + jnp.arange(per_brick, dtype=jnp.int32))
    return (inverted(incoming, per_brick), leaving, back, place)


def down(row):
    return jnp.broadcast_to(row, (128, 128)).T


def times(mat_ref, vec):
    total = [jnp.zeros((8, 128), F32) for _ in range(NB)]
    for i in range(NB):
        column = down(vec[i : i + 1, :])
        for j in range(NB):
            part = mat_ref[i * 128 : (i + 1) * 128, j * 128 : (j + 1) * 128] * column
            total[j] = total[j] + part.reshape(16, 8, 128).sum(axis=0)
    return jnp.concatenate([t.sum(axis=0, keepdims=True) for t in total], axis=0)


WIDTH = 1024
CHUNKS = COLS // WIDTH
NT = (((1,), (1,)), ((), ()))


def flat_rows(ref, chunk):
    count = WIDTH // 128
    rows = [ref[chunk * count + k : chunk * count + k + 1, :] for k in range(count)]
    return jnp.concatenate(rows, axis=1)


class Columns:
    def __init__(self, pieces, full_ref, sems):
        self.full_ref = full_ref
        self.copies = []
        for chunk in range(CHUNKS):
            to = pl.ds(chunk * WIDTH, WIDTH)
            self.copies.append(
                [
                    pltpu.make_async_copy(
                        piece.at[:, to], full_ref.at[k, :, to], sems.at[chunk, k]
                    )
                    for k, piece in enumerate(pieces)
                ]
            )
        for group in self.copies:
            for copy in group:
                copy.start()

    def chunk(self, chunk):
        for copy in self.copies[chunk]:
            copy.wait()
        return self.full_ref[:, :, chunk * WIDTH : (chunk + 1) * WIDTH].reshape(M, WIDTH)


def slots(at_ref):
    return [lax.rem(at_ref[0] + NB - k, NB) for k in range(NB)]


def as_rows(at_ref, lam_ref):
    flat = jnp.concatenate([lam_ref[pl.ds(slot, 1), :] for slot in slots(at_ref)], axis=1)
    return jnp.broadcast_to(flat, (16, M)).astype(BF)


def trial_chunk(block, curv_ref, lin_ref, lam_b, chunk):
    pushed = jnp.dot(lam_b, block, preferred_element_type=F32)
    curv, lin = flat_rows(curv_ref, chunk), flat_rows(lin_ref, chunk)
    return jnp.clip(-curv * (lin + pushed), -move_limit, move_limit)


def product_of_trial(at_ref, columns, curv_ref, lin_ref, lam_ref, part_ref):
    lam_b = as_rows(at_ref, lam_ref)
    total = jnp.zeros((16, M), F32)
    for chunk in range(CHUNKS):
        block = columns.chunk(chunk)
        moved = trial_chunk(block, curv_ref, lin_ref, lam_b, chunk).astype(BF)
        total += lax.dot_general(moved, block, NT, preferred_element_type=F32)
    for k, slot in enumerate(slots(at_ref)):
        part_ref[pl.ds(slot, 1), :] = total[0:1, k * 128 : (k + 1) * 128]


def newton_update(lam, total, bound, inv_ref, scale):
    rhs = (total * (1.0 / NVAR) - bound) * scale
    return jnp.maximum(lam + times(inv_ref, rhs) * scale, 0.0)


def packed_tile(p, t):
    tile = p * 16 + t
    shard, row = tile // (SHARD_G // 8), tile % (SHARD_G // 8) * 8
    return shard // HALF, shard % HALF, slice(row, row + 8)


def gram_kernel(
    at_ref, own_hbm, one_hbm, two_hbm, three_hbm, curv_ref, lin_ref,
    mine_ref, other_ref, gram_ref, prod_ref, block_ref, half_ref, full_ref, sems,
):
    core = at_ref[1]
    columns = Columns((own_hbm, one_hbm, two_hbm, three_hbm), full_ref, sems)
    gram_ref[...] = jnp.zeros_like(gram_ref)
    prod_ref[...] = jnp.zeros_like(prod_ref)
    for s in range(SHARDS):
        half_ref[s // HALF, s % HALF, SHARD_G:, :] = jnp.zeros((8, 128), F32)
    for chunk in range(CHUNKS):
        block = columns.chunk(chunk)
        curv, lin = flat_rows(curv_ref, chunk), flat_rows(lin_ref, chunk)
        weighted = (block.astype(F32) * curv).astype(BF)
        gram_ref[...] += lax.dot_general(weighted, block, NT, preferred_element_type=F32)
        moved = jnp.clip(-curv * lin, -move_limit, move_limit)
        moved = jnp.broadcast_to(moved, (16, WIDTH)).astype(BF)
        prod_ref[...] += lax.dot_general(moved, block, NT, preferred_element_type=F32)
    where = slots(at_ref)
    for a in range(NB):
        half_ref[0, pl.ds(where[a], 1), SHARD_G, :] = prod_ref[0:1, a * 128 : (a + 1) * 128]
        for b in range(NB):
            block_ref[where[a], where[b]] = gram_ref[
                a * 128 : (a + 1) * 128, b * 128 : (b + 1) * 128
            ]
    for p, (i, j) in enumerate(PAIRS):
        value = 0.5 * (block_ref[i, j] + block_ref[j, i].T)
        for t in range(16):
            half_ref[packed_tile(p, t)] = value[t * 8 : t * 8 + 8]
    mine_ref[...] = half_ref[core]
    other_ref[...] = half_ref[1 - core]


def split(value):
    high = value.astype(BF)
    return high, (value - high.astype(F32)).astype(BF)


def split_in_three(value):
    high = value.astype(BF)
    middle, low = split(value - high.astype(F32))
    return high, middle, low


def solve_kernel(
    at_ref, own_hbm, one_hbm, two_hbm, three_hbm, mine_ref, other_ref, curv_ref, lin_ref, bound_ref,
    inv_ref, scale_ref, lam_ref, part_ref,
    half_ref, hess_ref, r_ref, full_ref, sems,
):
    columns = Columns((own_hbm, one_hbm, two_hbm, three_hbm), full_ref, sems)
    core = at_ref[1]
    half_ref[core] = mine_ref[...]
    half_ref[1 - core] = other_ref[...]
    for p, (i, j) in enumerate(PAIRS):
        for t in range(16):
            at = i * 128 + t * 8
            hess_ref[at : at + 8, j * 128 : (j + 1) * 128] = half_ref[packed_tile(p, t)] * (
                1.0 / NVAR
            )
    row_id = lax.broadcasted_iota(jnp.int32, (128, 128), 0)
    col_id = lax.broadcasted_iota(jnp.int32, (128, 128), 1)
    diagonal = row_id == col_id
    for i in range(NB):
        at = slice(i * 128, (i + 1) * 128)
        for j in range(i):
            hess_ref[j * 128 : (j + 1) * 128, at] = hess_ref[at, j * 128 : (j + 1) * 128].T
        values = jnp.sum(jnp.where(diagonal, hess_ref[at, at], 0.0), axis=0, keepdims=True)
        scale_ref[i : i + 1, :] = lax.rsqrt(values)
    scale = scale_ref[...]
    scale_row = jnp.concatenate([scale[i : i + 1, :] for i in range(NB)], axis=1)
    widest = jnp.zeros((1, M), F32)
    for i in range(NB):
        at = slice(i * 128, (i + 1) * 128)
        column = jnp.concatenate([down(scale[i : i + 1, :])] * NB, axis=1)
        rows = hess_ref[at, :] * column * scale_row
        hess_ref[at, :] = rows
        widest = widest + jnp.sum(jnp.abs(rows), axis=0, keepdims=True)
    alpha = 1.9 / jnp.max(widest)

    def eye():
        rid = lax.broadcasted_iota(jnp.int32, (M, M), 0)
        cid = lax.broadcasted_iota(jnp.int32, (M, M), 1)
        return (rid == cid).astype(F32)

    first = eye() - alpha * hess_ref[...]
    r_ref[...] = first
    inv_ref[...] = alpha * (eye() + first)

    def double(_, carry):
        r = r_ref[...].astype(BF)
        r2 = jnp.dot(r, r, preferred_element_type=F32)
        r_ref[...] = r2
        inv_ref[...] += jnp.dot(
            inv_ref[...].astype(BF), r2.astype(BF), preferred_element_type=F32
        )
        return carry

    lax.fori_loop(0, DOUBLINGS - 1, double, 0)

    def correct(precise):
        dot = functools.partial(jnp.dot, preferred_element_type=F32)
        x_high, x_low = split(inv_ref[...])
        h_high, h_low, h_rest = split_in_three(hess_ref[...])
        product = dot(h_high, x_high)
        if precise:
            product += dot(h_high, x_low) + (
                dot(h_low, x_high) + (dot(h_low, x_low) + dot(h_rest, x_high))
            )
        else:
            product += dot(h_low, x_high)
        residual = eye() - product
        size = jnp.sum(residual * residual)
        good = size < M

        @pl.when(good)
        def _():
            r_high, r_low = split(residual)
            step = dot(x_high, r_high)
            inv_ref[...] = x_high.astype(F32) + step
            if precise:
                inv_ref[...] += x_low.astype(F32)

            if precise:

                @pl.when(size > TINY)
                def _():
                    inv_ref[...] += dot(x_high, r_low) + dot(x_low, r_high)

        @pl.when(jnp.logical_not(good))
        def _():
            inv_ref[...] = alpha * eye()

        return size

    def correct_again(state):
        return state[0] + 1, correct(True)

    def unfinished(state):
        count, size = state
        return jnp.logical_and(jnp.logical_not(size < ACCEPT), count < MAX_CORRECT)

    correct(False)
    _, size = lax.while_loop(unfinished, correct_again, (jnp.int32(0), jnp.float32(2.0 * M)))

    @pl.when(jnp.logical_not(size < ACCEPT))
    def _():
        inv_ref[...] = hess_ref[...]
        cid = lax.broadcasted_iota(jnp.int32, (8, M), 1)

        def pivot(k, carry):
            row = inv_ref[pl.ds(k, 1), :]
            here = lax.broadcasted_iota(jnp.int32, (1, M), 1) == k
            inverse = 1.0 / jnp.sum(jnp.where(here, row, 0.0))
            row = jnp.where(here, 1.0, row) * inverse

            def sweep(b, inner):
                at = pl.multiple_of(b * 8, 8)
                rows = inv_ref[pl.ds(at, 8), :]
                factor = jnp.sum(jnp.where(cid == k, rows, 0.0), axis=1, keepdims=True)
                rows = jnp.where(cid == k, 0.0, rows) - factor * row
                rid = lax.broadcasted_iota(jnp.int32, (8, M), 0) + at
                inv_ref[pl.ds(at, 8), :] = jnp.where(rid == k, row, rows)
                return inner

            lax.fori_loop(0, M // 8, sweep, 0)
            return carry

        lax.fori_loop(0, M, pivot, 0)

    total = jnp.concatenate(
        [half_ref[0, j, SHARD_G : SHARD_G + 1, :] for j in range(NB)], axis=0
    )
    zero = jnp.zeros((NB, 128), F32)
    lam = newton_update(zero, total, bound_ref[...], inv_ref, scale)
    lam_ref[...] = lam
    product_of_trial(at_ref, columns, curv_ref, lin_ref, lam_ref, part_ref)


def updated(gathered_ref, lam_in_ref, bound_ref, inv_ref, scale_ref):
    total = jnp.sum(gathered_ref[...], axis=0)
    return newton_update(lam_in_ref[...], total, bound_ref[...], inv_ref, scale_ref[...])


def step_kernel(
    at_ref, own_hbm, one_hbm, two_hbm, three_hbm, inv_ref,
    gathered_ref, lam_in_ref, curv_ref, lin_ref, bound_ref, scale_ref,
    lam_ref, part_ref, full_ref, sems,
):
    columns = Columns((own_hbm, one_hbm, two_hbm, three_hbm), full_ref, sems)
    lam_ref[...] = updated(gathered_ref, lam_in_ref, bound_ref, inv_ref, scale_ref)
    product_of_trial(at_ref, columns, curv_ref, lin_ref, lam_ref, part_ref)


def last_kernel(
    at_ref, own_hbm, one_hbm, two_hbm, three_hbm, inv_ref,
    gathered_ref, lam_in_ref, curv_ref, lin_ref, bound_ref, scale_ref,
    lam_ref, step_ref, full_ref, sems,
):
    columns = Columns((own_hbm, one_hbm, two_hbm, three_hbm), full_ref, sems)
    lam_ref[...] = updated(gathered_ref, lam_in_ref, bound_ref, inv_ref, scale_ref)
    lam_b = as_rows(at_ref, lam_ref)
    count = WIDTH // 128
    for chunk in range(CHUNKS):
        moved = trial_chunk(columns.chunk(chunk), curv_ref, lin_ref, lam_b, chunk)
        lines = [moved[0:1, k * 128 : (k + 1) * 128] for k in range(count)]
        lines = jnp.concatenate(lines, axis=0)
        for copy in range(step_ref.shape[0]):
            step_ref[copy, chunk * count : (chunk + 1) * count, :] = lines


VM = pl.BlockSpec(memory_space=pltpu.VMEM)
HBM = pl.BlockSpec(memory_space=pltpu.HBM)
FULL = [pltpu.VMEM((NB, ROWS, COLS), BF), pltpu.SemaphoreType.DMA((CHUNKS, NB))]
SM = pl.BlockSpec(memory_space=pltpu.SMEM)


def sds(shape, dtype=F32):
    return jax.ShapeDtypeStruct(shape, dtype)


def call(kernel, ins, outs, scratch, mib):
    return pl.pallas_call(
        kernel,
        in_specs=ins,
        out_specs=[VM] * len(outs),
        out_shape=outs,
        scratch_shapes=scratch,
        compiler_params=pltpu.CompilerParams(vmem_limit_bytes=mib * MIB),
    )


def summed(part):
    near = from_everyone(part, NEAR).sum(axis=0)
    return from_everyone(near, FAR)


def on_device(gradients, perm, weights, linear, bound):
    here = lax.axis_index(BRICK)
    quarter = lax.axis_index("grp")
    core = lax.axis_index("brick_2")
    per_brick = gradients.shape[1] // 128
    at = jnp.stack([quarter, core]).astype(jnp.int32)

    both = jnp.concatenate([weights.reshape(1, BLKS, 128), linear.reshape(1, BLKS, 128)], axis=2)
    both = jnp.broadcast_to(both, (size_of(NEAR), BLKS, 256))
    both = lax.all_to_all(both, NEAR, 0, 0, tiled=True)

    pieces = [
        lax.dynamic_slice(gradients, (0, lax.rem(quarter + k, NB) * COLS), (ROWS, COLS))
        for k in range(NB)
    ]
    pieces = list(lax.optimization_barrier(tuple(pieces)))
    for k in (1, 3, 2):
        ring = [(i, (i + k) % NB) for i in range(NB)]
        pieces[k] = lax.ppermute(pieces[k], "grp", ring)

    incoming, leaving, back, place = layout_tables(perm, here, per_brick)
    incoming = lax.dynamic_slice_in_dim(incoming, quarter * BLKS, BLKS)
    place = lax.dynamic_slice_in_dim(place, quarter * BLKS, BLKS)
    both = both.reshape(-1, 256)[leaving]
    both = lax.all_to_all(both, FAR, 0, 0, tiled=True)
    both = both[incoming]
    curv, lin, back, place = lax.optimization_barrier((both[:, :128], both[:, 128:], back, place))

    packed = (HALF, SHARD, 128)
    mine, other = call(
        gram_kernel,
        [SM] + [HBM] * NB + [VM] * 2,
        [sds(packed), sds(packed)],
        [
            pltpu.VMEM((M, M), F32),
            pltpu.VMEM((16, M), F32),
            pltpu.VMEM((NB, NB, 128, 128), F32),
            pltpu.VMEM((2, *packed), F32),
            *FULL,
        ],
        24,
    )(at, *pieces, curv, lin)

    pieces = [pltpu.with_memory_space_constraint(piece, pltpu.HBM) for piece in pieces]

    swap = [(0, 1), (1, 0)]
    mine = mine + lax.ppermute(other, "brick_2", swap)
    shard = lax.all_to_all(mine, PLANE, 0, 0, tiled=True).sum(axis=0)
    shard = from_everyone(shard, "brick_1").sum(axis=0)
    mine = from_everyone(shard, PLANE)
    other = lax.ppermute(mine, "brick_2", swap)

    bound = bound.reshape(NB, 128)
    square = sds((M, M))
    vector = sds((NB, 128))
    inv, scale, lam, part = call(
        solve_kernel,
        [SM] + [HBM] * NB + [VM] * 5,
        [square, vector, vector, vector],
        [
            pltpu.VMEM((2, *packed), F32),
            pltpu.VMEM((M, M), F32),
            pltpu.VMEM((M, M), F32),
            *FULL,
        ],
        32,
    )(at, *pieces, mine, other, curv, lin, bound)
    ins = [SM] + [HBM] * NB + [VM] * 7
    for _ in range(ITERS - 2):
        lam, part = call(step_kernel, ins, [vector, vector], FULL, 20)(
            at, *pieces, inv, summed(part), lam, curv, lin, bound, scale
        )
    lam, result = call(last_kernel, ins, [vector, sds((size_of(NEAR), BLKS, 128))], FULL, 20)(
        at, *pieces, inv, summed(part), lam, curv, lin, bound, scale
    )

    whole = lax.all_to_all(result, NEAR, 0, 0, tiled=True).reshape(-1, 128)
    arrived = lax.all_to_all(whole[back], FAR, 0, 0, tiled=True)
    return (arrived[place].reshape(-1), lam.reshape(-1))


def solution(mesh):
    torus = Mesh(
        mesh.devices.reshape(4, 8, 2, mesh.shape["grp"]), ("brick_0", "brick_1", "brick_2", "grp")
    )
    placed = (P("grp", BRICK), P(), P(BRICK_GRP), P(BRICK_GRP), P())
    return jax.shard_map(
        on_device, mesh=torus, in_specs=placed, out_specs=(P(BRICK_GRP), P()), check_vma=False
    )
```

```python
import functools

import jax
import jax.numpy as jnp
from jax import lax
from jax.experimental import pallas as pl
from jax.experimental.pallas import tpu as pltpu
from jax.sharding import Mesh
from jax.sharding import PartitionSpec as P


ITERS = 4
BRICK = ("brick_0", "brick_1", "brick_2")
BRICK_GRP = ("brick_0", "brick_1", "brick_2", "grp")
FAR = ("brick_0", "brick_1")
NEAR = ("brick_2", "grp")
PLANE = ("brick_0", "grp")
M = 512
ROWS = 128
NB = M // ROWS
COLS = 4096
BLKS = COLS // 128
NVAR = 1048576
PAIRS = [(i, j) for i in range(NB) for j in range(i + 1)]
SHARDS = 32
SHARD_G = len(PAIRS) * ROWS // SHARDS
SHARD = SHARD_G + 8
HALF = SHARDS // 2
DOUBLINGS = 4
MAX_CORRECT = 48
ACCEPT = 1e-4
TINY = 1e-5

move_limit = 1.0
MIB = 1024 * 1024
BF = jnp.bfloat16
F32 = jnp.float32


def size_of(axis):
    return lax.axis_size(axis)


def from_everyone(array, axis):
    devices = size_of(axis)
    return lax.all_to_all(
        jnp.broadcast_to(array[None], (devices, *array.shape)), axis, 0, 0, tiled=True
    )


def two_of(mask, values):
    index = lax.broadcasted_iota(jnp.int32, values.shape, 1)
    first = jnp.min(jnp.where(mask, index, values.shape[1]), axis=1, keepdims=True)
    second = jnp.max(jnp.where(mask, index, -1), axis=1, keepdims=True)
    kept = [jnp.sum(jnp.where(index == at, values, 0), axis=1) for at in (first, second)]
    return jnp.stack(kept, axis=1)


def ranks(keys):
    return jnp.sum(keys[None, :] < keys[:, None], axis=1, dtype=jnp.int32)


def inverted(places, count):
    slots = jnp.arange(count, dtype=jnp.int32)
    index = jnp.arange(places.shape[0], dtype=jnp.int32)
    return jnp.sum(jnp.where(places[None, :] == slots[:, None], index[None, :], 0), axis=1)


def layout_tables(perm, here, per_brick):
    chip, core = here // 2, here % 2
    per_chip = 2 * per_brick
    grid = perm.reshape(-1, per_brick)
    same = lax.dynamic_index_in_dim(grid.reshape(-1, 2, per_brick), core, 1, keepdims=False)
    rows = jnp.concatenate([grid, same, same], axis=0)
    bricks, chips = grid.shape[0], same.shape[0]
    line = lax.broadcasted_iota(jnp.int32, rows.shape, 0)
    wanted = jnp.where(line < bricks, here, chip * 2 + (line >= bricks + chips))
    picked = two_of(rows // per_brick == wanted, rows)
    incoming = picked[:bricks].reshape(-1) % per_brick
    back = jnp.stack([picked[bricks : bricks + chips], picked[bricks + chips :]], axis=1)
    back = back.reshape(-1) % per_chip
    local = lax.dynamic_slice_in_dim(perm, chip * per_chip, per_chip)
    index = jnp.arange(per_chip, dtype=jnp.int32)
    key = (local // per_chip) * per_chip + index
    key = jnp.where((local // per_brick) % 2 == core, key, key + perm.shape[0] * 2)
    leaving = inverted(ranks(key), per_brick)
    mine = lax.dynamic_slice_in_dim(perm, here * per_brick, per_brick)
    place = ranks((mine // per_brick) * per_brick + jnp.arange(per_brick, dtype=jnp.int32))
    return (inverted(incoming, per_brick), leaving, back, place)


def down(row):
    return jnp.broadcast_to(row, (128, 128)).T


def times(mat_ref, vec):
    total = [jnp.zeros((8, 128), F32) for _ in range(NB)]
    for i in range(NB):
        column = down(vec[i : i + 1, :])
        for j in range(NB):
            part = mat_ref[i * 128 : (i + 1) * 128, j * 128 : (j + 1) * 128] * column
            total[j] = total[j] + part.reshape(16, 8, 128).sum(axis=0)
    return jnp.concatenate([t.sum(axis=0, keepdims=True) for t in total], axis=0)


WIDTH = 1024
CHUNKS = COLS // WIDTH
NT = (((1,), (1,)), ((), ()))


def flat_rows(ref, chunk):
    count = WIDTH // 128
    rows = [ref[chunk * count + k : chunk * count + k + 1, :] for k in range(count)]
    return jnp.concatenate(rows, axis=1)


class Columns:
    def __init__(self, pieces, full_ref, sems):
        self.full_ref = full_ref
        self.copies = []
        for chunk in range(CHUNKS):
            to = pl.ds(chunk * WIDTH, WIDTH)
            self.copies.append(
                [
                    pltpu.make_async_copy(
                        piece.at[:, to], full_ref.at[k, :, to], sems.at[chunk, k]
                    )
                    for k, piece in enumerate(pieces)
                ]
            )
        for group in self.copies:
            for copy in group:
                copy.start()

    def chunk(self, chunk):
        for copy in self.copies[chunk]:
            copy.wait()
        return self.full_ref[:, :, chunk * WIDTH : (chunk + 1) * WIDTH].reshape(M, WIDTH)


def slots(at_ref):
    return [lax.rem(at_ref[0] + NB - k, NB) for k in range(NB)]


def as_rows(at_ref, lam_ref):
    flat = jnp.concatenate([lam_ref[pl.ds(slot, 1), :] for slot in slots(at_ref)], axis=1)
    return jnp.broadcast_to(flat, (16, M)).astype(BF)


def trial_chunk(block, curv_ref, lin_ref, lam_b, chunk):
    pushed = jnp.dot(lam_b, block, preferred_element_type=F32)
    curv, lin = flat_rows(curv_ref, chunk), flat_rows(lin_ref, chunk)
    return jnp.clip(-curv * (lin + pushed), -move_limit, move_limit)


def product_chunk(block, moved):
    moved = jnp.concatenate([moved.astype(BF)] * 8, axis=0)
    return lax.dot_general(block, moved, NT, preferred_element_type=F32)


def product_of_trial(at_ref, columns, curv_ref, lin_ref, lam_ref, part_ref):
    lam_b = as_rows(at_ref, lam_ref)
    total = jnp.zeros((M, 128), F32)
    for chunk in range(CHUNKS):
        block = columns.chunk(chunk)
        total += product_chunk(block, trial_chunk(block, curv_ref, lin_ref, lam_b, chunk))
    for k, slot in enumerate(slots(at_ref)):
        part_ref[pl.ds(slot, 1), :] = total[k * 128 : (k + 1) * 128, :].T[0:1, :]


def newton_update(lam, total, bound, inv_ref, scale):
    rhs = (total * (1.0 / NVAR) - bound) * scale
    return jnp.maximum(lam + times(inv_ref, rhs) * scale, 0.0)


def packed_tile(p, t):
    tile = p * 16 + t
    shard, row = tile // (SHARD_G // 8), tile % (SHARD_G // 8) * 8
    return shard // HALF, shard % HALF, slice(row, row + 8)


def gram_kernel(
    at_ref, own_hbm, one_hbm, two_hbm, three_hbm, curv_ref, lin_ref,
    mine_ref, other_ref, gram_ref, prod_ref, block_ref, half_ref, full_ref, sems,
):
    core = at_ref[1]
    columns = Columns((own_hbm, one_hbm, two_hbm, three_hbm), full_ref, sems)
    gram_ref[...] = jnp.zeros_like(gram_ref)
    prod_ref[...] = jnp.zeros_like(prod_ref)
    for s in range(SHARDS):
        half_ref[s // HALF, s % HALF, SHARD_G:, :] = jnp.zeros((8, 128), F32)
    for chunk in range(CHUNKS):
        block = columns.chunk(chunk)
        curv, lin = flat_rows(curv_ref, chunk), flat_rows(lin_ref, chunk)
        weighted = (block.astype(F32) * curv).astype(BF)
        gram_ref[...] += lax.dot_general(weighted, block, NT, preferred_element_type=F32)
        moved = jnp.clip(-curv * lin, -move_limit, move_limit)
        prod_ref[...] += product_chunk(block, jnp.broadcast_to(moved, (16, WIDTH)))
    where = slots(at_ref)
    for a in range(NB):
        line = prod_ref[a * 128 : (a + 1) * 128, :].T[0:1, :]
        half_ref[0, pl.ds(where[a], 1), SHARD_G, :] = line
        for b in range(NB):
            block_ref[where[a], where[b]] = gram_ref[
                a * 128 : (a + 1) * 128, b * 128 : (b + 1) * 128
            ]
    for p, (i, j) in enumerate(PAIRS):
        value = 0.5 * (block_ref[i, j] + block_ref[j, i].T)
        for t in range(16):
            half_ref[packed_tile(p, t)] = value[t * 8 : t * 8 + 8]
    mine_ref[...] = half_ref[core]
    other_ref[...] = half_ref[1 - core]


def split(value):
    high = value.astype(BF)
    return high, (value - high.astype(F32)).astype(BF)


def split_in_three(value):
    high = value.astype(BF)
    middle, low = split(value - high.astype(F32))
    return high, middle, low


def solve_kernel(
    at_ref, own_hbm, one_hbm, two_hbm, three_hbm, mine_ref, other_ref, curv_ref, lin_ref, bound_ref,
    inv_ref, scale_ref, lam_ref, part_ref,
    half_ref, hess_ref, r_ref, full_ref, sems,
):
    columns = Columns((own_hbm, one_hbm, two_hbm, three_hbm), full_ref, sems)
    core = at_ref[1]
    half_ref[core] = mine_ref[...]
    half_ref[1 - core] = other_ref[...]
    for p, (i, j) in enumerate(PAIRS):
        for t in range(16):
            at = i * 128 + t * 8
            hess_ref[at : at + 8, j * 128 : (j + 1) * 128] = half_ref[packed_tile(p, t)] * (
                1.0 / NVAR
            )
    row_id = lax.broadcasted_iota(jnp.int32, (128, 128), 0)
    col_id = lax.broadcasted_iota(jnp.int32, (128, 128), 1)
    diagonal = row_id == col_id
    for i in range(NB):
        at = slice(i * 128, (i + 1) * 128)
        for j in range(i):
            hess_ref[j * 128 : (j + 1) * 128, at] = hess_ref[at, j * 128 : (j + 1) * 128].T
        values = jnp.sum(jnp.where(diagonal, hess_ref[at, at], 0.0), axis=0, keepdims=True)
        scale_ref[i : i + 1, :] = lax.rsqrt(values)
    scale = scale_ref[...]
    scale_row = jnp.concatenate([scale[i : i + 1, :] for i in range(NB)], axis=1)
    widest = jnp.zeros((1, M), F32)
    for i in range(NB):
        at = slice(i * 128, (i + 1) * 128)
        column = jnp.concatenate([down(scale[i : i + 1, :])] * NB, axis=1)
        rows = hess_ref[at, :] * column * scale_row
        hess_ref[at, :] = rows
        widest = widest + jnp.sum(jnp.abs(rows), axis=0, keepdims=True)
    alpha = 1.9 / jnp.max(widest)

    def eye():
        rid = lax.broadcasted_iota(jnp.int32, (M, M), 0)
        cid = lax.broadcasted_iota(jnp.int32, (M, M), 1)
        return (rid == cid).astype(F32)

    first = eye() - alpha * hess_ref[...]
    r_ref[...] = first
    inv_ref[...] = alpha * (eye() + first)

    def double(_, carry):
        r = r_ref[...].astype(BF)
        r2 = jnp.dot(r, r, preferred_element_type=F32)
        r_ref[...] = r2
        inv_ref[...] += jnp.dot(
            inv_ref[...].astype(BF), r2.astype(BF), preferred_element_type=F32
        )
        return carry

    lax.fori_loop(0, DOUBLINGS - 1, double, 0)

    def correct(precise):
        dot = functools.partial(jnp.dot, preferred_element_type=F32)
        x_high, x_low = split(inv_ref[...])
        h_high, h_low, h_rest = split_in_three(hess_ref[...])
        product = dot(h_high, x_high)
        if precise:
            product += dot(h_high, x_low) + (
                dot(h_low, x_high) + (dot(h_low, x_low) + dot(h_rest, x_high))
            )
        else:
            product += dot(h_low, x_high)
        residual = eye() - product
        size = jnp.sum(residual * residual)
        good = size < M

        @pl.when(good)
        def _():
            r_high, r_low = split(residual)
            step = dot(x_high, r_high)
            inv_ref[...] = x_high.astype(F32) + step
            if precise:
                inv_ref[...] += x_low.astype(F32)

            if precise:

                @pl.when(size > TINY)
                def _():
                    inv_ref[...] += dot(x_high, r_low) + dot(x_low, r_high)

        @pl.when(jnp.logical_not(good))
        def _():
            inv_ref[...] = alpha * eye()

        return size

    def correct_again(state):
        return state[0] + 1, correct(True)

    def unfinished(state):
        count, size = state
        return jnp.logical_and(jnp.logical_not(size < ACCEPT), count < MAX_CORRECT)

    correct(False)
    _, size = lax.while_loop(unfinished, correct_again, (jnp.int32(0), jnp.float32(2.0 * M)))

    @pl.when(jnp.logical_not(size < ACCEPT))
    def _():
        inv_ref[...] = hess_ref[...]
        cid = lax.broadcasted_iota(jnp.int32, (8, M), 1)

        def pivot(k, carry):
            row = inv_ref[pl.ds(k, 1), :]
            here = lax.broadcasted_iota(jnp.int32, (1, M), 1) == k
            inverse = 1.0 / jnp.sum(jnp.where(here, row, 0.0))
            row = jnp.where(here, 1.0, row) * inverse

            def sweep(b, inner):
                at = pl.multiple_of(b * 8, 8)
                rows = inv_ref[pl.ds(at, 8), :]
                factor = jnp.sum(jnp.where(cid == k, rows, 0.0), axis=1, keepdims=True)
                rows = jnp.where(cid == k, 0.0, rows) - factor * row
                rid = lax.broadcasted_iota(jnp.int32, (8, M), 0) + at
                inv_ref[pl.ds(at, 8), :] = jnp.where(rid == k, row, rows)
                return inner

            lax.fori_loop(0, M // 8, sweep, 0)
            return carry

        lax.fori_loop(0, M, pivot, 0)

    total = jnp.concatenate(
        [half_ref[0, j, SHARD_G : SHARD_G + 1, :] for j in range(NB)], axis=0
    )
    zero = jnp.zeros((NB, 128), F32)
    lam = newton_update(zero, total, bound_ref[...], inv_ref, scale)
    lam_ref[...] = lam
    product_of_trial(at_ref, columns, curv_ref, lin_ref, lam_ref, part_ref)


def updated(gathered_ref, lam_in_ref, bound_ref, inv_ref, scale_ref):
    total = jnp.sum(gathered_ref[...], axis=0)
    return newton_update(lam_in_ref[...], total, bound_ref[...], inv_ref, scale_ref[...])


def step_kernel(
    at_ref, own_hbm, one_hbm, two_hbm, three_hbm, inv_ref,
    gathered_ref, lam_in_ref, curv_ref, lin_ref, bound_ref, scale_ref,
    lam_ref, part_ref, full_ref, sems,
):
    columns = Columns((own_hbm, one_hbm, two_hbm, three_hbm), full_ref, sems)
    lam_ref[...] = updated(gathered_ref, lam_in_ref, bound_ref, inv_ref, scale_ref)
    product_of_trial(at_ref, columns, curv_ref, lin_ref, lam_ref, part_ref)


def last_kernel(
    at_ref, own_hbm, one_hbm, two_hbm, three_hbm, inv_ref,
    gathered_ref, lam_in_ref, curv_ref, lin_ref, bound_ref, scale_ref,
    lam_ref, step_ref, full_ref, sems,
):
    columns = Columns((own_hbm, one_hbm, two_hbm, three_hbm), full_ref, sems)
    lam_ref[...] = updated(gathered_ref, lam_in_ref, bound_ref, inv_ref, scale_ref)
    lam_b = as_rows(at_ref, lam_ref)
    count = WIDTH // 128
    for chunk in range(CHUNKS):
        moved = trial_chunk(columns.chunk(chunk), curv_ref, lin_ref, lam_b, chunk)
        lines = [moved[0:1, k * 128 : (k + 1) * 128] for k in range(count)]
        lines = jnp.concatenate(lines, axis=0)
        for copy in range(step_ref.shape[0]):
            step_ref[copy, chunk * count : (chunk + 1) * count, :] = lines


VM = pl.BlockSpec(memory_space=pltpu.VMEM)
HBM = pl.BlockSpec(memory_space=pltpu.HBM)
FULL = [pltpu.VMEM((NB, ROWS, COLS), BF), pltpu.SemaphoreType.DMA((CHUNKS, NB))]
SM = pl.BlockSpec(memory_space=pltpu.SMEM)


def sds(shape, dtype=F32):
    return jax.ShapeDtypeStruct(shape, dtype)


def call(kernel, ins, outs, scratch, mib):
    return pl.pallas_call(
        kernel,
        in_specs=ins,
        out_specs=[VM] * len(outs),
        out_shape=outs,
        scratch_shapes=scratch,
        compiler_params=pltpu.CompilerParams(vmem_limit_bytes=mib * MIB),
    )


def summed(part):
    near = from_everyone(part, NEAR).sum(axis=0)
    return from_everyone(near, FAR)


def on_device(gradients, perm, weights, linear, bound):
    here = lax.axis_index(BRICK)
    quarter = lax.axis_index("grp")
    core = lax.axis_index("brick_2")
    per_brick = gradients.shape[1] // 128
    at = jnp.stack([quarter, core]).astype(jnp.int32)

    both = jnp.concatenate([weights.reshape(1, BLKS, 128), linear.reshape(1, BLKS, 128)], axis=2)
    both = jnp.broadcast_to(both, (size_of(NEAR), BLKS, 256))
    both = lax.all_to_all(both, NEAR, 0, 0, tiled=True)

    pieces = [
        lax.dynamic_slice(gradients, (0, lax.rem(quarter + k, NB) * COLS), (ROWS, COLS))
        for k in range(NB)
    ]
    pieces = list(lax.optimization_barrier(tuple(pieces)))
    for k in (1, 3, 2):
        ring = [(i, (i + k) % NB) for i in range(NB)]
        pieces[k] = lax.ppermute(pieces[k], "grp", ring)

    incoming, leaving, back, place = layout_tables(perm, here, per_brick)
    incoming = lax.dynamic_slice_in_dim(incoming, quarter * BLKS, BLKS)
    place = lax.dynamic_slice_in_dim(place, quarter * BLKS, BLKS)
    both = both.reshape(-1, 256)[leaving]
    both = lax.all_to_all(both, FAR, 0, 0, tiled=True)
    both = both[incoming]
    curv, lin, back, place = lax.optimization_barrier((both[:, :128], both[:, 128:], back, place))

    packed = (HALF, SHARD, 128)
    mine, other = call(
        gram_kernel,
        [SM] + [HBM] * NB + [VM] * 2,
        [sds(packed), sds(packed)],
        [
            pltpu.VMEM((M, M), F32),
            pltpu.VMEM((M, 128), F32),
            pltpu.VMEM((NB, NB, 128, 128), F32),
            pltpu.VMEM((2, *packed), F32),
            *FULL,
        ],
        24,
    )(at, *pieces, curv, lin)

    pieces = [pltpu.with_memory_space_constraint(piece, pltpu.HBM) for piece in pieces]
    *pieces, mine, other = lax.optimization_barrier((*pieces, mine, other))

    swap = [(0, 1), (1, 0)]
    mine = mine + lax.ppermute(other, "brick_2", swap)
    shard = lax.all_to_all(mine, PLANE, 0, 0, tiled=True).sum(axis=0)
    shard = from_everyone(shard, "brick_1").sum(axis=0)
    mine = from_everyone(shard, PLANE)
    other = lax.ppermute(mine, "brick_2", swap)

    bound = bound.reshape(NB, 128)
    square = sds((M, M))
    vector = sds((NB, 128))
    inv, scale, lam, part = call(
        solve_kernel,
        [SM] + [HBM] * NB + [VM] * 5,
        [square, vector, vector, vector],
        [
            pltpu.VMEM((2, *packed), F32),
            pltpu.VMEM((M, M), F32),
            pltpu.VMEM((M, M), F32),
            *FULL,
        ],
        32,
    )(at, *pieces, mine, other, curv, lin, bound)
    ins = [SM] + [HBM] * NB + [VM] * 7
    for _ in range(ITERS - 2):
        lam, part = call(step_kernel, ins, [vector, vector], FULL, 20)(
            at, *pieces, inv, summed(part), lam, curv, lin, bound, scale
        )
    lam, result = call(last_kernel, ins, [vector, sds((size_of(NEAR), BLKS, 128))], FULL, 20)(
        at, *pieces, inv, summed(part), lam, curv, lin, bound, scale
    )

    whole = lax.all_to_all(result, NEAR, 0, 0, tiled=True).reshape(-1, 128)
    arrived = lax.all_to_all(whole[back], FAR, 0, 0, tiled=True)
    return (arrived[place].reshape(-1), lam.reshape(-1))


def solution(mesh):
    torus = Mesh(
        mesh.devices.reshape(4, 8, 2, mesh.shape["grp"]), ("brick_0", "brick_1", "brick_2", "grp")
    )
    placed = (P("grp", BRICK), P(), P(BRICK_GRP), P(BRICK_GRP), P())
    return jax.shard_map(
        on_device, mesh=torus, in_specs=placed, out_specs=(P(BRICK_GRP), P()), check_vma=False
    )
```

```python
import functools

import jax
import jax.numpy as jnp
from jax import lax
from jax.experimental import pallas as pl
from jax.experimental.pallas import tpu as pltpu
from jax.sharding import Mesh
from jax.sharding import PartitionSpec as P


ITERS = 4
BRICK = ("brick_0", "brick_1", "brick_2")
BRICK_GRP = ("brick_0", "brick_1", "brick_2", "grp")
FAR = ("brick_0", "brick_1")
NEAR = ("brick_2", "grp")
PLANE = ("brick_0", "grp")
M = 512
ROWS = 128
NB = M // ROWS
COLS = 4096
BLKS = COLS // 128
NVAR = 1048576
PAIRS = [(i, j) for i in range(NB) for j in range(i + 1)]
SHARDS = 32
SHARD_G = len(PAIRS) * ROWS // SHARDS
SHARD = SHARD_G + 8
HALF = SHARDS // 2
DOUBLINGS = 4
MAX_CORRECT = 48
ACCEPT = 1e-4
TINY = 1e-5

move_limit = 1.0
MIB = 1024 * 1024
BF = jnp.bfloat16
F32 = jnp.float32


def size_of(axis):
    return lax.axis_size(axis)


def from_everyone(array, axis):
    devices = size_of(axis)
    return lax.all_to_all(
        jnp.broadcast_to(array[None], (devices, *array.shape)), axis, 0, 0, tiled=True
    )


def two_of(mask, values):
    index = lax.broadcasted_iota(jnp.int32, values.shape, 1)
    first = jnp.min(jnp.where(mask, index, values.shape[1]), axis=1, keepdims=True)
    second = jnp.max(jnp.where(mask, index, -1), axis=1, keepdims=True)
    kept = [jnp.sum(jnp.where(index == at, values, 0), axis=1) for at in (first, second)]
    return jnp.stack(kept, axis=1)


def ranks(keys):
    return jnp.sum(keys[None, :] < keys[:, None], axis=1, dtype=jnp.int32)


def inverted(places, count):
    slots = jnp.arange(count, dtype=jnp.int32)
    index = jnp.arange(places.shape[0], dtype=jnp.int32)
    return jnp.sum(jnp.where(places[None, :] == slots[:, None], index[None, :], 0), axis=1)


def layout_tables(perm, here, per_brick):
    chip, core = here // 2, here % 2
    per_chip = 2 * per_brick
    grid = perm.reshape(-1, per_brick)
    same = lax.dynamic_index_in_dim(grid.reshape(-1, 2, per_brick), core, 1, keepdims=False)
    rows = jnp.concatenate([grid, same, same], axis=0)
    bricks, chips = grid.shape[0], same.shape[0]
    line = lax.broadcasted_iota(jnp.int32, rows.shape, 0)
    wanted = jnp.where(line < bricks, here, chip * 2 + (line >= bricks + chips))
    picked = two_of(rows // per_brick == wanted, rows)
    incoming = picked[:bricks].reshape(-1) % per_brick
    back = jnp.stack([picked[bricks : bricks + chips], picked[bricks + chips :]], axis=1)
    back = back.reshape(-1) % per_chip
    local = lax.dynamic_slice_in_dim(perm, chip * per_chip, per_chip)
    index = jnp.arange(per_chip, dtype=jnp.int32)
    key = (local // per_chip) * per_chip + index
    key = jnp.where((local // per_brick) % 2 == core, key, key + perm.shape[0] * 2)
    leaving = inverted(ranks(key), per_brick)
    mine = lax.dynamic_slice_in_dim(perm, here * per_brick, per_brick)
    place = ranks((mine // per_brick) * per_brick + jnp.arange(per_brick, dtype=jnp.int32))
    return (inverted(incoming, per_brick), leaving, back, place)


def down(row):
    return jnp.broadcast_to(row, (128, 128)).T


def times(mat_ref, vec):
    total = [jnp.zeros((8, 128), F32) for _ in range(NB)]
    for i in range(NB):
        column = down(vec[i : i + 1, :])
        for j in range(NB):
            part = mat_ref[i * 128 : (i + 1) * 128, j * 128 : (j + 1) * 128] * column
            total[j] = total[j] + part.reshape(16, 8, 128).sum(axis=0)
    return jnp.concatenate([t.sum(axis=0, keepdims=True) for t in total], axis=0)


WIDTH = 1024
CHUNKS = COLS // WIDTH
NT = (((1,), (1,)), ((), ()))


def flat_rows(ref, chunk):
    count = WIDTH // 128
    rows = [ref[chunk * count + k : chunk * count + k + 1, :] for k in range(count)]
    return jnp.concatenate(rows, axis=1)


class Columns:
    def __init__(self, pieces, full_ref, sems):
        self.full_ref = full_ref
        self.copies = []
        for chunk in range(CHUNKS):
            to = pl.ds(chunk * WIDTH, WIDTH)
            self.copies.append(
                [
                    pltpu.make_async_copy(
                        piece.at[:, to], full_ref.at[k, :, to], sems.at[chunk, k]
                    )
                    for k, piece in enumerate(pieces)
                ]
            )
        for group in self.copies:
            for copy in group:
                copy.start()

    def chunk(self, chunk):
        for copy in self.copies[chunk]:
            copy.wait()
        return self.full_ref[:, :, chunk * WIDTH : (chunk + 1) * WIDTH].reshape(M, WIDTH)


def slots(at_ref):
    return [lax.rem(at_ref[0] + NB - k, NB) for k in range(NB)]


def as_rows(at_ref, lam_ref):
    flat = jnp.concatenate([lam_ref[pl.ds(slot, 1), :] for slot in slots(at_ref)], axis=1)
    return jnp.broadcast_to(flat, (16, M)).astype(BF)


def trial_chunk(block, curv_ref, lin_ref, lam_b, chunk):
    pushed = jnp.dot(lam_b, block, preferred_element_type=F32)
    curv, lin = flat_rows(curv_ref, chunk), flat_rows(lin_ref, chunk)
    return jnp.clip(-curv * (lin + pushed), -move_limit, move_limit)


def product_of_trial(at_ref, columns, curv_ref, lin_ref, lam_ref, part_ref):
    lam_b = as_rows(at_ref, lam_ref)
    total = jnp.zeros((16, M), F32)
    for chunk in range(CHUNKS):
        block = columns.chunk(chunk)
        moved = trial_chunk(block, curv_ref, lin_ref, lam_b, chunk).astype(BF)
        total += lax.dot_general(moved, block, NT, preferred_element_type=F32)
    for k, slot in enumerate(slots(at_ref)):
        part_ref[pl.ds(slot, 1), :] = total[0:1, k * 128 : (k + 1) * 128]


def newton_update(lam, total, bound, inv_ref, scale):
    rhs = (total * (1.0 / NVAR) - bound) * scale
    return jnp.maximum(lam + times(inv_ref, rhs) * scale, 0.0)


def packed_tile(p, t):
    tile = p * 16 + t
    shard, row = tile // (SHARD_G // 8), tile % (SHARD_G // 8) * 8
    return shard // HALF, shard % HALF, slice(row, row + 8)


def gram_kernel(
    at_ref, own_hbm, one_hbm, two_hbm, three_hbm, curv_ref, lin_ref,
    mine_ref, other_ref, gram_ref, block_ref, half_ref, full_ref, sems,
):
    core = at_ref[1]
    columns = Columns((own_hbm, one_hbm, two_hbm, three_hbm), full_ref, sems)
    gram_ref[...] = jnp.zeros_like(gram_ref)
    for s in range(SHARDS):
        half_ref[s // HALF, s % HALF, SHARD_G:, :] = jnp.zeros((8, 128), F32)
    for chunk in range(CHUNKS):
        block = columns.chunk(chunk)
        curv, lin = flat_rows(curv_ref, chunk), flat_rows(lin_ref, chunk)
        weighted = (block.astype(F32) * curv).astype(BF)
        moved = jnp.clip(-curv * lin, -move_limit, move_limit)
        moved = jnp.broadcast_to(moved, (16, WIDTH)).astype(BF)
        both = jnp.concatenate([weighted, moved], axis=0)
        gram_ref[...] += lax.dot_general(both, block, NT, preferred_element_type=F32)
    where = slots(at_ref)
    for a in range(NB):
        half_ref[0, pl.ds(where[a], 1), SHARD_G, :] = gram_ref[M : M + 1, a * 128 : (a + 1) * 128]
        for b in range(NB):
            block_ref[where[a], where[b]] = gram_ref[
                a * 128 : (a + 1) * 128, b * 128 : (b + 1) * 128
            ]
    for p, (i, j) in enumerate(PAIRS):
        value = 0.5 * (block_ref[i, j] + block_ref[j, i].T)
        for t in range(16):
            half_ref[packed_tile(p, t)] = value[t * 8 : t * 8 + 8]
    mine_ref[...] = half_ref[core]
    other_ref[...] = half_ref[1 - core]


def split(value):
    high = value.astype(BF)
    return high, (value - high.astype(F32)).astype(BF)


def split_in_three(value):
    high = value.astype(BF)
    middle, low = split(value - high.astype(F32))
    return high, middle, low


def solve_kernel(
    at_ref, own_hbm, one_hbm, two_hbm, three_hbm, mine_ref, other_ref, curv_ref, lin_ref, bound_ref,
    inv_ref, scale_ref, lam_ref, part_ref,
    half_ref, hess_ref, r_ref, full_ref, sems,
):
    columns = Columns((own_hbm, one_hbm, two_hbm, three_hbm), full_ref, sems)
    core = at_ref[1]
    half_ref[core] = mine_ref[...]
    half_ref[1 - core] = other_ref[...]
    for p, (i, j) in enumerate(PAIRS):
        for t in range(16):
            at = i * 128 + t * 8
            hess_ref[at : at + 8, j * 128 : (j + 1) * 128] = half_ref[packed_tile(p, t)] * (
                1.0 / NVAR
            )
    row_id = lax.broadcasted_iota(jnp.int32, (128, 128), 0)
    col_id = lax.broadcasted_iota(jnp.int32, (128, 128), 1)
    diagonal = row_id == col_id
    for i in range(NB):
        at = slice(i * 128, (i + 1) * 128)
        for j in range(i):
            hess_ref[j * 128 : (j + 1) * 128, at] = hess_ref[at, j * 128 : (j + 1) * 128].T
        values = jnp.sum(jnp.where(diagonal, hess_ref[at, at], 0.0), axis=0, keepdims=True)
        scale_ref[i : i + 1, :] = lax.rsqrt(values)
    scale = scale_ref[...]
    scale_row = jnp.concatenate([scale[i : i + 1, :] for i in range(NB)], axis=1)
    widest = jnp.zeros((1, M), F32)
    for i in range(NB):
        at = slice(i * 128, (i + 1) * 128)
        column = jnp.concatenate([down(scale[i : i + 1, :])] * NB, axis=1)
        rows = hess_ref[at, :] * column * scale_row
        hess_ref[at, :] = rows
        widest = widest + jnp.sum(jnp.abs(rows), axis=0, keepdims=True)
    alpha = 1.9 / jnp.max(widest)

    def eye():
        rid = lax.broadcasted_iota(jnp.int32, (M, M), 0)
        cid = lax.broadcasted_iota(jnp.int32, (M, M), 1)
        return (rid == cid).astype(F32)

    first = eye() - alpha * hess_ref[...]
    r_ref[...] = first
    inv_ref[...] = alpha * (eye() + first)

    def double(_, carry):
        r = r_ref[...].astype(BF)
        r2 = jnp.dot(r, r, preferred_element_type=F32)
        r_ref[...] = r2
        inv_ref[...] += jnp.dot(
            inv_ref[...].astype(BF), r2.astype(BF), preferred_element_type=F32
        )
        return carry

    lax.fori_loop(0, DOUBLINGS - 1, double, 0)

    def correct(precise):
        dot = functools.partial(jnp.dot, preferred_element_type=F32)
        x_high, x_low = split(inv_ref[...])
        h_high, h_low, h_rest = split_in_three(hess_ref[...])
        product = dot(h_high, x_high)
        if precise:
            product += dot(h_high, x_low) + (
                dot(h_low, x_high) + (dot(h_low, x_low) + dot(h_rest, x_high))
            )
        else:
            product += dot(h_low, x_high)
        residual = eye() - product
        size = jnp.sum(residual * residual)
        good = size < M

        @pl.when(good)
        def _():
            r_high, r_low = split(residual)
            step = dot(x_high, r_high)
            inv_ref[...] = x_high.astype(F32) + step
            if precise:
                inv_ref[...] += x_low.astype(F32)

            if precise:

                @pl.when(size > TINY)
                def _():
                    inv_ref[...] += dot(x_high, r_low) + dot(x_low, r_high)

        @pl.when(jnp.logical_not(good))
        def _():
            inv_ref[...] = alpha * eye()

        return size

    def correct_again(state):
        return state[0] + 1, correct(True)

    def unfinished(state):
        count, size = state
        return jnp.logical_and(jnp.logical_not(size < ACCEPT), count < MAX_CORRECT)

    correct(False)
    _, size = lax.while_loop(unfinished, correct_again, (jnp.int32(0), jnp.float32(2.0 * M)))

    @pl.when(jnp.logical_not(size < ACCEPT))
    def _():
        inv_ref[...] = hess_ref[...]
        cid = lax.broadcasted_iota(jnp.int32, (8, M), 1)

        def pivot(k, carry):
            row = inv_ref[pl.ds(k, 1), :]
            here = lax.broadcasted_iota(jnp.int32, (1, M), 1) == k
            inverse = 1.0 / jnp.sum(jnp.where(here, row, 0.0))
            row = jnp.where(here, 1.0, row) * inverse

            def sweep(b, inner):
                at = pl.multiple_of(b * 8, 8)
                rows = inv_ref[pl.ds(at, 8), :]
                factor = jnp.sum(jnp.where(cid == k, rows, 0.0), axis=1, keepdims=True)
                rows = jnp.where(cid == k, 0.0, rows) - factor * row
                rid = lax.broadcasted_iota(jnp.int32, (8, M), 0) + at
                inv_ref[pl.ds(at, 8), :] = jnp.where(rid == k, row, rows)
                return inner

            lax.fori_loop(0, M // 8, sweep, 0)
            return carry

        lax.fori_loop(0, M, pivot, 0)

    total = jnp.concatenate(
        [half_ref[0, j, SHARD_G : SHARD_G + 1, :] for j in range(NB)], axis=0
    )
    zero = jnp.zeros((NB, 128), F32)
    lam = newton_update(zero, total, bound_ref[...], inv_ref, scale)
    lam_ref[...] = lam
    product_of_trial(at_ref, columns, curv_ref, lin_ref, lam_ref, part_ref)


def updated(gathered_ref, lam_in_ref, bound_ref, inv_ref, scale_ref):
    total = jnp.sum(gathered_ref[...], axis=0)
    return newton_update(lam_in_ref[...], total, bound_ref[...], inv_ref, scale_ref[...])


def step_kernel(
    at_ref, own_hbm, one_hbm, two_hbm, three_hbm, inv_ref,
    gathered_ref, lam_in_ref, curv_ref, lin_ref, bound_ref, scale_ref,
    lam_ref, part_ref, full_ref, sems,
):
    columns = Columns((own_hbm, one_hbm, two_hbm, three_hbm), full_ref, sems)
    lam_ref[...] = updated(gathered_ref, lam_in_ref, bound_ref, inv_ref, scale_ref)
    product_of_trial(at_ref, columns, curv_ref, lin_ref, lam_ref, part_ref)


def last_kernel(
    at_ref, own_hbm, one_hbm, two_hbm, three_hbm, inv_ref,
    gathered_ref, lam_in_ref, curv_ref, lin_ref, bound_ref, scale_ref,
    lam_ref, step_ref, full_ref, sems,
):
    columns = Columns((own_hbm, one_hbm, two_hbm, three_hbm), full_ref, sems)
    lam_ref[...] = updated(gathered_ref, lam_in_ref, bound_ref, inv_ref, scale_ref)
    lam_b = as_rows(at_ref, lam_ref)
    count = WIDTH // 128
    for chunk in range(CHUNKS):
        moved = trial_chunk(columns.chunk(chunk), curv_ref, lin_ref, lam_b, chunk)
        lines = [moved[0:1, k * 128 : (k + 1) * 128] for k in range(count)]
        lines = jnp.concatenate(lines, axis=0)
        for copy in range(step_ref.shape[0]):
            step_ref[copy, chunk * count : (chunk + 1) * count, :] = lines


VM = pl.BlockSpec(memory_space=pltpu.VMEM)
HBM = pl.BlockSpec(memory_space=pltpu.HBM)
FULL = [pltpu.VMEM((NB, ROWS, COLS), BF), pltpu.SemaphoreType.DMA((CHUNKS, NB))]
SM = pl.BlockSpec(memory_space=pltpu.SMEM)


def sds(shape, dtype=F32):
    return jax.ShapeDtypeStruct(shape, dtype)


def call(kernel, ins, outs, scratch, mib):
    return pl.pallas_call(
        kernel,
        in_specs=ins,
        out_specs=[VM] * len(outs),
        out_shape=outs,
        scratch_shapes=scratch,
        compiler_params=pltpu.CompilerParams(vmem_limit_bytes=mib * MIB),
    )


def summed(part):
    near = from_everyone(part, NEAR).sum(axis=0)
    return from_everyone(near, FAR)


def on_device(gradients, perm, weights, linear, bound):
    here = lax.axis_index(BRICK)
    quarter = lax.axis_index("grp")
    core = lax.axis_index("brick_2")
    per_brick = gradients.shape[1] // 128
    at = jnp.stack([quarter, core]).astype(jnp.int32)

    both = jnp.concatenate([weights.reshape(1, BLKS, 128), linear.reshape(1, BLKS, 128)], axis=2)
    both = jnp.broadcast_to(both, (size_of(NEAR), BLKS, 256))
    both = lax.all_to_all(both, NEAR, 0, 0, tiled=True)

    pieces = [
        lax.dynamic_slice(gradients, (0, lax.rem(quarter + k, NB) * COLS), (ROWS, COLS))
        for k in range(NB)
    ]
    pieces = list(lax.optimization_barrier(tuple(pieces)))
    for k in (1, 3, 2):
        ring = [(i, (i + k) % NB) for i in range(NB)]
        pieces[k] = lax.ppermute(pieces[k], "grp", ring)

    incoming, leaving, back, place = layout_tables(perm, here, per_brick)
    incoming = lax.dynamic_slice_in_dim(incoming, quarter * BLKS, BLKS)
    place = lax.dynamic_slice_in_dim(place, quarter * BLKS, BLKS)
    both = both.reshape(-1, 256)[leaving]
    both = lax.all_to_all(both, FAR, 0, 0, tiled=True)
    both = both[incoming]
    curv, lin, back, place = lax.optimization_barrier((both[:, :128], both[:, 128:], back, place))

    packed = (HALF, SHARD, 128)
    mine, other = call(
        gram_kernel,
        [SM] + [HBM] * NB + [VM] * 2,
        [sds(packed), sds(packed)],
        [
            pltpu.VMEM((M + 16, M), F32),
            pltpu.VMEM((NB, NB, 128, 128), F32),
            pltpu.VMEM((2, *packed), F32),
            *FULL,
        ],
        24,
    )(at, *pieces, curv, lin)

    pieces = [pltpu.with_memory_space_constraint(piece, pltpu.HBM) for piece in pieces]

    swap = [(0, 1), (1, 0)]
    mine = mine + lax.ppermute(other, "brick_2", swap)
    shard = lax.all_to_all(mine, PLANE, 0, 0, tiled=True).sum(axis=0)
    shard = from_everyone(shard, "brick_1").sum(axis=0)
    mine = from_everyone(shard, PLANE)
    other = lax.ppermute(mine, "brick_2", swap)

    bound = bound.reshape(NB, 128)
    square = sds((M, M))
    vector = sds((NB, 128))
    inv, scale, lam, part = call(
        solve_kernel,
        [SM] + [HBM] * NB + [VM] * 5,
        [square, vector, vector, vector],
        [
            pltpu.VMEM((2, *packed), F32),
            pltpu.VMEM((M, M), F32),
            pltpu.VMEM((M, M), F32),
            *FULL,
        ],
        32,
    )(at, *pieces, mine, other, curv, lin, bound)
    ins = [SM] + [HBM] * NB + [VM] * 7
    for _ in range(ITERS - 2):
        lam, part = call(step_kernel, ins, [vector, vector], FULL, 20)(
            at, *pieces, inv, summed(part), lam, curv, lin, bound, scale
        )
    lam, result = call(last_kernel, ins, [vector, sds((size_of(NEAR), BLKS, 128))], FULL, 20)(
        at, *pieces, inv, summed(part), lam, curv, lin, bound, scale
    )

    whole = lax.all_to_all(result, NEAR, 0, 0, tiled=True).reshape(-1, 128)
    arrived = lax.all_to_all(whole[back], FAR, 0, 0, tiled=True)
    return (arrived[place].reshape(-1), lam.reshape(-1))


def solution(mesh):
    torus = Mesh(
        mesh.devices.reshape(4, 8, 2, mesh.shape["grp"]), ("brick_0", "brick_1", "brick_2", "grp")
    )
    placed = (P("grp", BRICK), P(), P(BRICK_GRP), P(BRICK_GRP), P())
    return jax.shard_map(
        on_device, mesh=torus, in_specs=placed, out_specs=(P(BRICK_GRP), P()), check_vma=False
    )
```
